32 devices in a mesh: ctx: 16 (over z, y, x), section: 2 (over core).
Axes of the slice: x: 2, y: 2, z: 4, core: 2. Of those that a mesh axis runs over, the one named last changes fastest.
Arguments:
- layer_inputs: bfloat16 [2, 4096, 1536], P('section', 'ctx'), may hold values from -6 to 6
- conv_weight: bfloat16 [2, 3, 1536, 768], P('section', None, 'ctx'), may hold values from -0.09375 to 0.09375
- mix_weight: bfloat16 [2, 768, 1536], P('section', 'ctx'), may hold values from -0.21875 to 0.21875
- bn_scale: float32 [2, 1536], P('section'), may hold values from 0.5 to 2
- bn_shift: float32 [2, 1536], P('section'), may hold values from -4 to 4
- cotangent: bfloat16 [4096, 1536], P('ctx'), may hold values from -6 to 6
Outputs:
- input_grads: bfloat16 [2, 4096, 1536], P('section', 'ctx')
The draws below stay inside these ranges and needn't reach their ends.
All inputs are finite; a program needn't handle non-finite values.
Results may differ from the reference program's by a relative error of at most 0.0053.
Values may be sent and summed in bfloat16 or wider, within the bound.
A program may use at most 64 MiB of HBM per device.

```python
import math
import jax
import jax.numpy as jnp
from jax import lax

C = 1536
H = 768
TAPS = 3
POSITIONS = 4096
LAYERS = 2


def levels(rng, extent, cuts, low, largest):
    def one(dim, blocks):
        draws = jax.random.uniform(jax.random.fold_in(jax.random.fold_in(rng, 6), dim), (blocks,), jnp.float32, low / len(cuts), largest / len(cuts))
        return jnp.repeat(jnp.exp(draws), extent[dim] // blocks).reshape((-1,) + (1,) * (len(extent) - dim - 1))

    loudness = one(*cuts[0])
    for cut in cuts[1:]:
        loudness = loudness * one(*cut)
    return loudness


def noise(key, dims, scale, most, cuts=(), held_as=jnp.bfloat16):
    entries = jax.random.normal(key, dims, jnp.float32) * scale
    if len(cuts) > 0:
        entries = levels(key, dims, cuts, -0.22, 0.18) * entries
    return jnp.clip(entries, min=-most, max=most).astype(held_as)


def setup_inputs(seed: int = 0) -> dict:
    key_list = jax.random.split(jax.random.key(seed), 7)
    layer_inputs = noise(key_list[0], (LAYERS, POSITIONS, C), 1.0, 6.0, ((0, 2), (1, 16)))
    conv_weight = noise(key_list[1], (LAYERS, TAPS, C, H), (3 * C) ** -0.5, 0.09375, ((0, 2), (2, 16)))
    mix_weight = noise(key_list[2], (LAYERS, H, C), H ** -0.5, 0.21875, ((0, 2), (1, 16)))
    bn_scale = jnp.clip(jnp.exp(math.log(2.0) - 1.3862944 * jax.random.uniform(key_list[3], (LAYERS, C), jnp.float32) ** levels(key_list[3], (LAYERS, C), ((0, 2),), -0.2, 0.2)), 0.5, 2.0)
    bn_shift = noise(key_list[4], (LAYERS, C), 1.0, 4.0, ((0, 2),), jnp.float32)
    cotangent = noise(key_list[5], (POSITIONS, C), 1.0, 6.0, ((0, 16),))
    return {"layer_inputs": layer_inputs, "conv_weight": conv_weight, "mix_weight": mix_weight, "bn_scale": bn_scale, "bn_shift": bn_shift, "cotangent": cotangent}


def gelu_parts(value):
    cdf = 0.5 * (1.0 + lax.erf(value * 0.7071067811865476))
    dens = jnp.exp(-0.5 * value * value) * 0.3989422804014327
    return value * cdf, cdf + value * dens


def reference(layer_inputs, conv_weight, mix_weight, bn_scale, bn_shift, cotangent):
    sections = layer_inputs.shape[0]
    total = layer_inputs.shape[1]
    grad = cotangent
    results = [None] * sections
    for level in reversed(range(sections)):
        spacing = 2 ** level
        pre = layer_inputs[level].astype(jnp.float32) * bn_scale[level] + bn_shift[level]
        act, slope_pre = gelu_parts(pre)
        hidden = act.astype(jnp.bfloat16)
        padded = jnp.pad(hidden, ((spacing, spacing), (0, 0)))
        conv = jnp.zeros((total, conv_weight.shape[3]), jnp.float32)
        for k in range(3):
            conv = conv + jnp.dot(padded[k * spacing:k * spacing + total], conv_weight[level, k], preferred_element_type=jnp.float32)
        _, slope_conv = gelu_parts(conv)
        back = jnp.dot(grad, mix_weight[level].T, preferred_element_type=jnp.float32)
        dconv = (back * slope_conv).astype(jnp.bfloat16)
        dpad = jnp.pad(dconv, ((spacing, spacing), (0, 0)))
        dhidden = jnp.zeros((total, conv_weight.shape[2]), jnp.float32)
        for k in range(3):
            begin = (2 - k) * spacing
            dhidden = dhidden + jnp.dot(dpad[begin:begin + total], conv_weight[level, k].T, preferred_element_type=jnp.float32)
        grad = (grad.astype(jnp.float32) + dhidden * slope_pre * bn_scale[level]).astype(jnp.bfloat16)
        results[level] = grad
    return jnp.stack(results)
```

```python
import jax
import jax.numpy as jnp
from jax import lax
from jax.experimental import pallas as pl
from jax.experimental.pallas import tpu as pltpu
from jax.sharding import PartitionSpec as P

MESH = pl.DeviceIdType.MESH
EDGE = 16
LANES = 128
TILE = 256
DEVICES = 32
GATE = 1
BEHIND = 2


def mate(level, c):
    return level * (c + 1 - 2 * (c % 2)) + (1 - level) * (c + 2 - 4 * ((c // 2) % 2))


class Spot:
    def __init__(self):
        self.level = level = lax.axis_index("section")
        self.me = me = lax.axis_index("ctx")
        y, x = (me // 2) % 2, me % 2
        self.z = me // 4
        self.p = level * x + (1 - level) * y
        self.q = level * y + (1 - level) * x

    def ctx(self, z, q, p):
        return z * 4 + self.level * (2 * q + p) + (1 - self.level) * (2 * p + q)


def greet(spot):
    barrier = pltpu.get_barrier_semaphore()
    index = spot.me * 2 + spot.level

    def hello(k, c):
        device = (index + k) % DEVICES
        pl.semaphore_signal(
            barrier, inc=1, device_id={"ctx": device // 2, "section": device % 2}, device_id_type=MESH
        )
        return c

    lax.fori_loop(1, DEVICES, hello, 0)
    pl.semaphore_wait(barrier, DEVICES - 1)


PAIR, SIDE, UP, DOWN = range(4)
OUTER, LAST, MIX = range(3)


class Gather:
    def __init__(self, spot, conv, mix, conv_full, mix_full, send_sem, recv_sem, own_sem):
        self.spot, self.conv, self.mix, self.conv_full, self.mix_full = spot, conv, mix, conv_full, mix_full
        self.send_sem, self.recv_sem, self.own_sem = send_sem, recv_sem, own_sem
        self.depth, self.inner = conv.shape[2], mix.shape[1]
        self.half = conv_full.shape[2]

    def own(self, kind, p):
        cols = pl.ds(pl.multiple_of(p * self.half, 128), self.half)
        if kind == OUTER:
            return self.conv.at[0, pl.ds(0, 2), :, cols]
        if kind == LAST:
            return self.conv.at[0, 2, :, cols]
        return self.mix.at[0]

    def full(self, kind, source):
        rows = pl.ds(pl.multiple_of(source * self.depth, 16), self.depth)
        if kind == OUTER:
            return self.conv_full.at[pl.ds(0, 2), rows, :]
        if kind == LAST:
            return self.conv_full.at[2, rows, :]
        return self.mix_full.at[pl.ds(pl.multiple_of((source % 8) * self.inner, 16), self.inner), :]

    def copy(self, kind, source, mine, lane):
        spot = self.spot
        z, q, p = spot.z, spot.q, spot.p
        device = (
            spot.ctx(z, q, 1 - p), spot.ctx(z, 1 - q, p), spot.ctx(z + 1, q, p), spot.ctx(z - 1, q, p),
        )[lane]
        here = self.full(kind, source)
        if mine:
            here = self.own(kind, 1 - p if lane == PAIR else p)
        return pltpu.make_async_remote_copy(
            src_ref=here,
            dst_ref=self.full(kind, source),
            send_sem=self.send_sem.at[kind, source, lane],
            recv_sem=self.recv_sem.at[kind, source],
            device_id={"ctx": device},
            device_id_type=MESH,
        )

    def send(self, kind, source, mine, lane, act):
        z = self.spot.z
        if lane == UP:
            pl.when(z < 3)(lambda: act(self.copy(kind, source, mine, lane)))
        elif lane == DOWN:
            pl.when(z > 0)(lambda: act(self.copy(kind, source, mine, lane)))
        else:
            act(self.copy(kind, source, mine, lane))

    def local(self, kind):
        return pltpu.make_async_copy(
            self.own(kind, self.spot.p), self.full(kind, self.spot.me), self.own_sem.at[kind]
        )

    def mixes(self, z, p, body):
        pl.when(z // 2 == p)(body)

    def begin(self, act):
        spot = self.spot
        me, z, p = spot.me, spot.z, spot.p
        for lane in (UP, DOWN):
            self.send(OUTER, me, True, lane, act)
        self.send(OUTER, me, True, PAIR, act)
        self.send(LAST, me, True, SIDE, act)
        self.send(LAST, me, True, PAIR, act)

        @pl.when(z // 2 == 1 - p)
        def _():
            self.send(MIX, me, True, PAIR, act)

        @pl.when(z // 2 == p)
        def _():
            for lane in (UP, DOWN, SIDE):
                self.send(MIX, me, True, lane, act)

        for lane in (UP, DOWN):
            self.send(LAST, me, True, lane, act)
        self.send(OUTER, me, True, SIDE, act)

    def onward(self, kind, source, t, sign, act):
        if t == 0:
            self.send(kind, source, False, UP, act)
            self.send(kind, source, False, DOWN, act)
        else:

            @pl.when(sign < 0)
            def _():
                self.send(kind, source, False, UP, act)

            @pl.when(sign > 0)
            def _():
                self.send(kind, source, False, DOWN, act)

    def arrive(self, kind, source):
        self.copy(kind, source, False, PAIR).wait_recv()

    def each(self, t, body):
        if t == 0:
            body(0)
            return
        z = self.spot.z

        def side(b, c):
            sign = 1 - 2 * b

            @pl.when((z + sign * t >= 0) & (z + sign * t < 4))
            def _():
                body(sign)

            return c

        lax.fori_loop(0, 2, side, 0)

    def hop(self, t, sign, act, wait):
        spot = self.spot
        z, q, p = spot.z + sign * t, spot.q, spot.p
        for dp in (0, 1):
            near = spot.ctx(z, q, 1 - p if dp else p)
            far = spot.ctx(z, 1 - q, 1 - p if dp else p)
            if t > 0 or dp > 0:
                if wait:
                    self.arrive(OUTER, near)
                self.onward(OUTER, near, t, sign, act)
                self.send(OUTER, near, False, SIDE, act)

                if wait:
                    self.arrive(LAST, near)
                self.onward(LAST, near, t, sign, act)
                if t == 0:
                    self.send(LAST, near, False, SIDE, act)

            if wait:
                self.arrive(LAST, far)
            self.onward(LAST, far, t, sign, act)
            if t > 0 or dp > 0:

                @pl.when(z // 2 == p)
                def _():
                    if wait:
                        self.arrive(MIX, near)
                    self.onward(MIX, near, t, sign, act)
                    self.send(MIX, near, False, SIDE, act)

    def rest(self, t, sign):
        spot = self.spot
        z = spot.z + sign * t
        for dp in (0, 1):
            far = spot.ctx(z, 1 - spot.q, 1 - spot.p if dp else spot.p)
            self.arrive(OUTER, far)

            @pl.when(z // 2 == spot.p)
            def _():
                self.arrive(MIX, far)


class Edges:
    def __init__(self, spot, level, source, first, buffer, send_sem, recv_sem):
        self.me, self.level, self.source, self.first, self.buffer = spot.me, level, source, first, buffer
        self.send_sem, self.recv_sem = send_sem, recv_sem
        self.rows = buffer.shape[1] - 2 * EDGE
        self.same = level is spot.level
        self.section = level

    def land(self, side, slot):
        return self.buffer.at[slot, pl.ds(0 if side == 0 else EDGE + self.rows, EDGE), :]

    def sends(self, remote, local):
        for side in (0, 1):
            there = self.me < 15 if side == 0 else self.me > 0
            near = self.me + 1 if side == 0 else self.me - 1
            for slot in (0, 1):
                target = near if slot == 0 else mate(self.level, near)
                start = self.first + (self.rows - EDGE if side == 0 else 0)
                source = self.source(start)
                copy = pltpu.make_async_remote_copy(
                    src_ref=source,
                    dst_ref=self.land(side, slot),
                    send_sem=self.send_sem.at[side, slot],
                    recv_sem=self.recv_sem.at[side, slot],
                    device_id={"ctx": target, "section": self.section},
                    device_id_type=MESH,
                )
                if slot == 0:
                    pl.when(there)(lambda: remote(copy))
                else:
                    pl.when(there & (target != self.me))(lambda: remote(copy))
                    if local is not None:
                        pl.when(there & (target == self.me))(
                            lambda: local(
                                pltpu.make_async_copy(source, self.land(side, slot), self.recv_sem.at[side, slot])
                            )
                        )

    def start(self):
        self.sends(lambda c: c.start(), lambda c: c.start())

    def sent(self):
        self.sends(lambda c: c.wait_send(), None)

    def receive(self):
        for slot in (0, 1):
            block = self.me if slot == 0 else mate(self.level, self.me)
            for side in (0, 1):
                there = block > 0 if side == 0 else block < 15
                giver = block - 1 if side == 0 else block + 1
                land = self.land(side, slot)
                source = self.buffer.at[0, pl.ds(EDGE, EDGE), :]

                @pl.when(there & (giver != self.me))
                def _():
                    pltpu.make_async_remote_copy(
                        src_ref=source,
                        dst_ref=land,
                        send_sem=self.send_sem.at[side, slot],
                        recv_sem=self.recv_sem.at[side, slot],
                        device_id={"ctx": giver},
                        device_id_type=MESH,
                    ).wait_recv()

                @pl.when(there & (giver == self.me))
                def _():
                    pltpu.make_async_copy(source, land, self.recv_sem.at[side, slot]).wait()

                @pl.when(jnp.logical_not(there))
                def _():
                    land[...] = jnp.zeros(land.shape, land.dtype)


def columns(count, width, body):
    def step(n, c):
        body(pl.ds(pl.multiple_of(n * width, width), width), n)
        return c

    lax.fori_loop(0, count, step, 0)


def across(left, right):
    return lax.dot_general(left, right, (((1,), (1,)), ((), ())), preferred_element_type=jnp.float32)


def tower_kernel(
    conv_w, mix_w, inputs, scale, shift, cotangent, out,
    conv_full, mix_full, held, factor, hidden, grad, conv_sum, back, dpadded, dconv, dtotal, part_out, part_in, result,
    send_sem, recv_sem, own_sem, load_sem, hid_send, hid_recv, edge_send, edge_recv, cot_send, cot_recv, cedge_send, cedge_recv,
    grad_send, grad_recv, gedge_send, gedge_recv, part_send, part_recv, out_sem, gate,
):
    spot = Spot()
    level, me = spot.level, spot.me
    rows, wide = cotangent.shape
    half = conv_full.shape[2]
    plane = wide // 4
    tall = rows + 2 * EDGE
    tiles = wide // TILE
    middle = pl.ds(EDGE, rows)
    partner = spot.ctx(spot.z, spot.q, 1 - spot.p)
    gather = Gather(spot, conv_w, mix_w, conv_full, mix_full, send_sem, recv_sem, own_sem)

    def start(copy):
        copy.start()

    load = pltpu.make_async_copy(inputs.at[0], held, load_sem.at[0])
    load.start()
    load_cot = pltpu.make_async_copy(cotangent, grad.at[0, middle, :], load_sem.at[1])
    pl.when(level == 1)(load_cot.start)
    for kind in (OUTER, LAST):
        gather.local(kind).start()
    gather.mixes(spot.z, spot.p, gather.local(MIX).start)
    greet(spot)

    def cot_copy():
        return pltpu.make_async_remote_copy(
            src_ref=cotangent, dst_ref=grad.at[1, middle, :], send_sem=cot_send, recv_sem=cot_recv,
            device_id={"ctx": partner}, device_id_type=MESH,
        )

    cot_edges = Edges(spot, level, lambda r: cotangent.at[pl.ds(r, EDGE), :], 0, grad, cedge_send, cedge_recv)

    @pl.when(level == 1)
    def _():
        gather.begin(start)
        cot_copy().start()
        cot_edges.start()

    load.wait()

    def front(cols, _):
        gain = scale[:, cols]
        pre = held[:, cols].astype(jnp.float32) * gain + shift[:, cols]
        act, slope = gelu_parts(pre)
        hidden[0, middle, cols] = act.astype(jnp.bfloat16)
        factor[:, cols] = slope * gain

    columns(wide // LANES, LANES, front)

    def hid_copy():
        return pltpu.make_async_remote_copy(
            src_ref=hidden.at[0, middle, :], dst_ref=hidden.at[1, middle, :], send_sem=hid_send, recv_sem=hid_recv,
            device_id={"ctx": partner}, device_id_type=MESH,
        )

    edges = Edges(spot, level, lambda r: hidden.at[0, pl.ds(r, EDGE), :], EDGE, hidden, edge_send, edge_recv)

    @pl.when(level == 0)
    def _():
        pl.semaphore_wait(gate, 1)
        gather.begin(start)

    hid_copy().start()
    edges.start()
    for kind in (OUTER, LAST):
        gather.local(kind).wait()
    gather.mixes(spot.z, spot.p, gather.local(MIX).wait)

    def add_plane(t):
        def body(sign):
            gather.rest(t, sign)
            off = pl.ds(pl.multiple_of((spot.z + sign * t) * plane, plane), plane)
            for k in range(3):

                def slot(n, c):
                    term = jnp.dot(hidden[n, :, off], conv_full[k, off, :], preferred_element_type=jnp.float32)
                    if t == 0:
                        conv_sum[k, n] = term
                    else:
                        conv_sum[k, n] += term
                    return c

                lax.fori_loop(0, 2, slot, 0)

        gather.each(t, body)

    def grad_copy(n, slot):
        cols = pl.ds(n * TILE, TILE)
        return pltpu.make_async_remote_copy(
            src_ref=result.at[:, cols],
            dst_ref=grad.at[slot, middle, cols],
            send_sem=grad_send.at[n, slot],
            recv_sem=grad_recv.at[n, slot],
            device_id={"ctx": me if slot == 0 else mate(0, me), "section": 0},
            device_id_type=MESH,
        )

    grad_edges = Edges(spot, 0, lambda r: result.at[pl.ds(r, EDGE), :], 0, grad, gedge_send, gedge_recv)

    for t in range(4):
        gather.each(t, lambda sign: gather.hop(t, sign, start, True))
        if t == GATE:

            @pl.when(level == 1)
            def _():
                pl.semaphore_signal(gate, inc=1, device_id={"section": 0}, device_id_type=MESH)

        if t == 1:
            hid_copy().wait_recv()
            edges.receive()
        if t > 0:
            add_plane(t - 1)
    add_plane(3)

    @pl.when(level == 1)
    def _():
        load_cot.wait()
        cot_copy().wait_recv()
        cot_edges.receive()

    @pl.when(level == 0)
    def _():
        for n in range(tiles):
            for slot in (0, 1):
                grad_copy(n, slot).wait_recv()
        grad_edges.receive()

    def pull(n, c):
        back[n] = across(grad[n], mix_full[...])
        return c

    lax.fori_loop(0, 2, pull, 0)

    low, count = EDGE // 2, rows + EDGE

    def slopes(cols, _):
        for n in range(2):
            near = conv_sum[0, n, low - 1:low - 1 + count, cols] + conv_sum[2, n, low + 1:low + 1 + count, cols]
            far = conv_sum[0, n, low - 2:low - 2 + count, cols] + conv_sum[2, n, low + 2:low + 2 + count, cols]
            conv = jnp.where(level == 0, near, far) + conv_sum[1, n, low:low + count, cols]
            value = back[n, low:low + count, cols] * gelu_parts(conv)[1]
            dpadded[n, low:low + count, cols] = value.astype(jnp.bfloat16).astype(jnp.float32)
            there = pl.ds(n * rows, rows)
            dconv[1, there, cols] = dpadded[n, EDGE:EDGE + rows, cols].astype(jnp.bfloat16)
            near = dpadded[n, EDGE + 1:EDGE + 1 + rows, cols]
            far = dpadded[n, EDGE + 2:EDGE + 2 + rows, cols]
            dconv[0, there, cols] = jnp.where(level == 0, near, far).astype(jnp.bfloat16)
            near = dpadded[n, EDGE - 1:EDGE - 1 + rows, cols]
            far = dpadded[n, EDGE - 2:EDGE - 2 + rows, cols]
            dconv[2, there, cols] = jnp.where(level == 0, near, far).astype(jnp.bfloat16)

    columns(half // LANES, LANES, slopes)

    def part_copy(n):
        return pltpu.make_async_remote_copy(
            src_ref=part_out.at[n], dst_ref=part_in.at[n], send_sem=part_send.at[n], recv_sem=part_recv.at[n],
            device_id={"ctx": partner}, device_id_type=MESH,
        )

    def out_copy(n):
        cols = pl.ds(n * TILE, TILE)
        return pltpu.make_async_copy(result.at[:, cols], out.at[0, :, cols], out_sem.at[n])

    for n in range(tiles + BEHIND):
        if n < tiles:
            cols = pl.ds(n * TILE, TILE)
            term = across(dconv[0], conv_full[0, cols, :])
            term += across(dconv[1], conv_full[1, cols, :])
            term += across(dconv[2], conv_full[2, cols, :])
            part_out[n] = term[rows:].astype(jnp.bfloat16)
            dtotal[:, cols] = term[:rows]
            part_copy(n).start()
        m = n - BEHIND
        if m >= 0:
            cols = pl.ds(m * TILE, TILE)
            part_copy(m).wait_recv()
            dhidden = dtotal[:, cols] + part_in[m].astype(jnp.float32)
            result[:, cols] = (
                grad[0, middle, cols].astype(jnp.float32) + dhidden * factor[:, cols]
            ).astype(jnp.bfloat16)
            out_copy(m).start()

            @pl.when(level == 1)
            def _():
                grad_copy(m, 0).start()
                grad_copy(m, 1).start()

    @pl.when(level == 1)
    def _():
        grad_edges.start()
        cot_copy().wait_send()
        cot_edges.sent()

    hid_copy().wait_send()
    edges.sent()
    gather.begin(lambda c: c.wait_send())
    for t in range(4):
        gather.each(t, lambda sign: gather.hop(t, sign, lambda c: c.wait_send(), False))
    for n in range(tiles):
        part_copy(n).wait_send()
        out_copy(n).wait()

    @pl.when(level == 1)
    def _():
        for n in range(tiles):
            for slot in (0, 1):
                grad_copy(n, slot).wait_send()
        grad_edges.sent()


def tower(layer_inputs, conv_weight, mix_weight, bn_scale, bn_shift, cotangent):
    rows, wide = cotangent.shape
    inner = conv_weight.shape[3]
    half = inner // 2
    tall = rows + 2 * EDGE
    tiles = wide // TILE
    anywhere = pl.BlockSpec(memory_space=pl.ANY)
    vmem = pl.BlockSpec(memory_space=pltpu.VMEM)
    bf16, f32 = jnp.bfloat16, jnp.float32
    dma = pltpu.SemaphoreType.DMA
    return pl.pallas_call(
        tower_kernel,
        out_shape=jax.ShapeDtypeStruct(layer_inputs.shape, bf16),
        in_specs=[anywhere, anywhere, anywhere, vmem, vmem, anywhere],
        out_specs=anywhere,
        scratch_shapes=[
            pltpu.VMEM((3, wide, half), bf16),
            pltpu.VMEM((half, wide), bf16),
            pltpu.VMEM((rows, wide), bf16),
            pltpu.VMEM((rows, wide), f32),
            pltpu.VMEM((2, tall, wide), bf16),
            pltpu.VMEM((2, tall, wide), bf16),
            pltpu.VMEM((3, 2, tall, half), f32),
            pltpu.VMEM((2, tall, half), f32),
            pltpu.VMEM((2, tall, half), f32),
            pltpu.VMEM((3, 2 * rows, half), bf16),
            pltpu.VMEM((rows, wide), f32),
            pltpu.VMEM((tiles, rows, TILE), bf16),
            pltpu.VMEM((tiles, rows, TILE), bf16),
            pltpu.VMEM((rows, wide), bf16),
            dma((3, 16, 4)),
            dma((3, 16)),
            dma((3,)),
            dma((2,)),
            dma,
            dma,
            dma((2, 2)),
            dma((2, 2)),
            dma,
            dma,
            dma((2, 2)),
            dma((2, 2)),
            dma((tiles, 2)),
            dma((tiles, 2)),
            dma((2, 2)),
            dma((2, 2)),
            dma((tiles,)),
            dma((tiles,)),
            dma((tiles,)),
            pltpu.SemaphoreType.REGULAR,
        ],
        compiler_params=pltpu.CompilerParams(
            collective_id=0, has_side_effects=True, vmem_limit_bytes=48 * 1024 * 1024
        ),
    )(conv_weight, mix_weight, layer_inputs, bn_scale, bn_shift, cotangent)


def extended(cells, sides, width):
    for axis, dim in sides:
        count = lax.axis_size(axis)
        ends = count - 1
        head = lax.slice_in_dim(cells, 0, width, axis=dim)
        tail = lax.slice_in_dim(cells, cells.shape[dim] - width, cells.shape[dim], axis=dim)
        cells = jnp.concatenate(
            [
                lax.ppermute(tail, axis, [(i, (i + 1) % count) for i in range(ends)]),
                cells,
                lax.ppermute(head, axis, [((i + 1) % count, i) for i in range(ends)]),
            ],
            axis=dim,
        )
    return cells


def shifted(block, axis, distance):
    devices = range(lax.axis_size(axis))
    route = [(i - distance, i) for i in devices if i - distance in devices]
    return lax.ppermute(block, axis, route)


def gelu_parts(value):
    cdf = 0.5 * (1.0 + lax.erf(value * 0.7071067811865476))
    dens = jnp.exp(-0.5 * value * value) * 0.3989422804014327
    return (value * cdf, cdf + value * dens)


def shards(layer_inputs, conv_weight, mix_weight, bn_scale, bn_shift, cotangent):
    sections = lax.axis_size("section")
    level = lax.axis_index("section")
    widest = 2 ** (sections - 1)
    if lax.axis_size("ctx") == 16 and sections == 2:
        return tower(layer_inputs, conv_weight, mix_weight, bn_scale, bn_shift, cotangent)
    conv_full = lax.all_gather(conv_weight, "ctx", axis=2, tiled=True)[0]
    mix_full = lax.all_gather(mix_weight, "ctx", axis=1, tiled=True)[0]
    rows = cotangent.shape[0]
    inner = mix_full.shape[0]
    spacing = jnp.left_shift(jnp.int32(1), level)
    pre = layer_inputs[0].astype(jnp.float32) * bn_scale[0] + bn_shift[0]
    act, slope_pre = gelu_parts(pre)
    hidden = act.astype(jnp.bfloat16)
    padded = extended(hidden, (("ctx", 0),), widest)
    conv = jnp.zeros((rows, inner), jnp.float32)
    for k in range(3):
        window = lax.dynamic_slice_in_dim(padded, widest + (k - 1) * spacing, rows, 0)
        conv = conv + jnp.dot(window, conv_full[k], preferred_element_type=jnp.float32)
    _, slope_conv = gelu_parts(conv)
    factor = slope_pre * bn_scale[0]

    def make_dconv(grad):
        back = jnp.einsum("pc,hc->ph", grad, mix_full, preferred_element_type=jnp.float32)
        return (back * slope_conv).astype(jnp.bfloat16)

    def skip_dconv(grad):
        return jnp.zeros((rows, inner), jnp.bfloat16)

    def finish(grad, dpad, starts):
        dhidden = jnp.zeros((rows, conv_full.shape[1]), jnp.float32)
        for k in range(3):
            window = lax.dynamic_slice_in_dim(dpad, starts[k], rows, 0)
            dhidden = dhidden + jnp.einsum(
                "ph,ch->pc", window, conv_full[k], preferred_element_type=jnp.float32
            )
        return (grad.astype(jnp.float32) + dhidden * factor).astype(jnp.bfloat16)

    mine = jnp.zeros_like(cotangent)

    def turn(step, carry):
        grad, mine = carry
        active = level == sections - 1 - step
        dconv = lax.cond(active, make_dconv, skip_dconv, grad)
        dpad = extended(dconv, (("ctx", 0),), widest)
        starts = [widest + (1 - k) * spacing for k in range(3)]
        result = lax.cond(active, lambda g: finish(g, dpad, starts), lambda g: g, grad)
        mine = jnp.where(active, result, mine)
        grad = shifted(result, "section", -1)
        return (grad, mine)

    grad, mine = lax.fori_loop(0, sections, turn, (cotangent, mine))
    return mine[None]


def solution(mesh):
    return jax.shard_map(
        shards,
        mesh=mesh,
        in_specs=(
            P("section", "ctx", None),
            P("section", None, "ctx", None),
            P("section", "ctx", None),
            P("section", None),
            P("section", None),
            P("ctx", None),
        ),
        out_specs=P("section", "ctx", None),
        check_vma=False,
    )
```

```python
import jax
import jax.numpy as jnp
from jax import lax
from jax.experimental import pallas as pl
from jax.experimental.pallas import tpu as pltpu
from jax.sharding import PartitionSpec as P

MESH = pl.DeviceIdType.MESH
EDGE = 16
LANES = 128
TILE = 256
DEVICES = 32
GATES = {"pair": 3, "ends": 1, "inner": 5}
BEHIND = 2


def mate(c):
    return c + 1 - 2 * (c % 2)


class Spot:
    def __init__(self):
        self.level = lax.axis_index("section")
        self.me = me = lax.axis_index("ctx")
        self.z, self.q, self.p = me // 4, (me // 2) % 2, me % 2

    def ctx(self, z, q, p):
        return z * 4 + q * 2 + p


def greet(spot):
    barrier = pltpu.get_barrier_semaphore()
    index = spot.me * 2 + spot.level

    def hello(k, c):
        device = (index + k) % DEVICES
        pl.semaphore_signal(
            barrier, inc=1, device_id={"ctx": device // 2, "section": device % 2}, device_id_type=MESH
        )
        return c

    lax.fori_loop(1, DEVICES, hello, 0)
    pl.semaphore_wait(barrier, DEVICES - 1)


PAIR, SIDE, UP, DOWN = range(4)
OUTER, LAST, MIX = range(3)


class Gather:
    def __init__(self, spot, conv, mix, conv_full, mix_full, other, send_sem, recv_sem, own_sem):
        self.spot, self.conv, self.mix, self.conv_full, self.mix_full = spot, conv, mix, conv_full, mix_full
        self.other, self.send_sem, self.recv_sem, self.own_sem = other, send_sem, recv_sem, own_sem
        self.depth, self.inner = conv.shape[2], mix.shape[1]
        self.half = conv_full.shape[1] // 3

    def taps(self, kind):
        return pl.ds(0, 2 * self.half) if kind == OUTER else pl.ds(2 * self.half, self.half)

    def full(self, kind, source):
        if kind != MIX:
            rows = pl.ds(pl.multiple_of(source * self.depth, 16), self.depth)
            return self.conv_full.at[rows, self.taps(kind)]
        return self.mix_full.at[pl.ds(pl.multiple_of((source % 8) * self.inner, 16), self.inner), :]

    def copy(self, kind, source, mine, lane):
        spot = self.spot
        z, q, p = spot.z, spot.q, spot.p
        device = (
            spot.ctx(z, q, 1 - p), spot.ctx(z, 1 - q, p), spot.ctx(z + 1, q, p), spot.ctx(z - 1, q, p),
        )[lane]
        here = self.full(kind, source)
        if mine and kind == MIX:
            here = self.mix.at[0]
        elif mine and lane == PAIR:
            here = self.other.at[:, self.taps(kind)]
        return pltpu.make_async_remote_copy(
            src_ref=here,
            dst_ref=self.full(kind, source),
            send_sem=self.send_sem.at[kind, source, lane],
            recv_sem=self.recv_sem.at[kind, source],
            device_id={"ctx": device},
            device_id_type=MESH,
        )

    def send(self, kind, source, mine, lane, act):
        z = self.spot.z
        if lane == UP:
            pl.when(z < 3)(lambda: act(self.copy(kind, source, mine, lane)))
        elif lane == DOWN:
            pl.when(z > 0)(lambda: act(self.copy(kind, source, mine, lane)))
        else:
            act(self.copy(kind, source, mine, lane))

    def own(self):
        spot = self.spot
        copies = []
        for k in range(3):
            for n, p in enumerate((spot.p, 1 - spot.p)):
                cols = pl.ds(k * self.half, self.half)
                rows = pl.ds(pl.multiple_of(spot.me * self.depth, 16), self.depth)
                copies.append(
                    pltpu.make_async_copy(
                        self.conv.at[0, k, :, pl.ds(pl.multiple_of(p * self.half, 128), self.half)],
                        self.other.at[:, cols] if n else self.conv_full.at[rows, cols],
                        self.own_sem.at[k, n],
                    )
                )
        return copies

    def own_mix(self, act):
        spot = self.spot
        pl.when(spot.z // 2 == spot.p)(
            lambda: act(pltpu.make_async_copy(self.mix.at[0], self.full(MIX, spot.me), self.own_sem.at[3, 0]))
        )

    def begin_pair(self, act):
        spot = self.spot
        self.send(OUTER, spot.me, True, PAIR, act)

        @pl.when(spot.z // 2 == 1 - spot.p)
        def _():
            self.send(MIX, spot.me, True, PAIR, act)

        self.send(LAST, spot.me, True, PAIR, act)

    def begin(self, act):
        spot = self.spot
        me = spot.me
        for lane in (UP, DOWN):
            self.send(OUTER, me, True, lane, act)
        self.send(LAST, me, True, SIDE, act)

        @pl.when(spot.z // 2 == spot.p)
        def _():
            for lane in (UP, DOWN, SIDE):
                self.send(MIX, me, True, lane, act)

        self.send(OUTER, me, True, SIDE, act)

    def onward(self, kind, source, t, sign, act):
        if t == 0:
            self.send(kind, source, False, UP, act)
            self.send(kind, source, False, DOWN, act)
        else:

            @pl.when(sign < 0)
            def _():
                self.send(kind, source, False, UP, act)

            @pl.when(sign > 0)
            def _():
                self.send(kind, source, False, DOWN, act)

    def arrive(self, kind, source):
        self.copy(kind, source, False, PAIR).wait_recv()

    def each(self, t, body):
        if t == 0:
            body(0)
            return
        z = self.spot.z

        def side(b, c):
            sign = 1 - 2 * b

            @pl.when((z + sign * t >= 0) & (z + sign * t < 4))
            def _():
                body(sign)

            return c

        lax.fori_loop(0, 2, side, 0)

    def hop(self, t, sign, act, wait):
        spot = self.spot
        z, q, p = spot.z + sign * t, spot.q, spot.p
        for dp in (0, 1) if t else (1,):
            near = spot.ctx(z, q, 1 - p if dp else p)
            if wait:
                self.arrive(OUTER, near)
            self.onward(OUTER, near, t, sign, act)
            self.send(OUTER, near, False, SIDE, act)

            @pl.when(z // 2 == p)
            def _():
                if wait:
                    self.arrive(MIX, near)
                self.onward(MIX, near, t, sign, act)
                self.send(MIX, near, False, SIDE, act)

            if t == 0:
                if wait:
                    self.arrive(LAST, near)
                self.send(LAST, near, False, SIDE, act)

    def hop_last(self, t, sign, act, wait):
        spot = self.spot
        z = spot.z + sign * t
        for q in (spot.q, 1 - spot.q):
            for p in (spot.p, 1 - spot.p):
                source = spot.ctx(z, q, p)
                if wait:
                    self.arrive(LAST, source)
                self.onward(LAST, source, t, sign, act)

    def launch_last(self, t, act, wait):
        spot = self.spot
        for lane, ready in ((DOWN, spot.z + t == 3), (UP, spot.z == t)):

            @pl.when(ready)
            def _():
                for q in (0, 1):
                    for p in (0, 1):
                        self.send(LAST, spot.ctx(spot.z, q, p), False, lane, act)

    def side_last(self):
        spot = self.spot
        for p in (0, 1):
            self.arrive(LAST, spot.ctx(spot.z, 1 - spot.q, p))

    def rest(self, z):
        spot = self.spot
        for p in (0, 1):
            far = spot.ctx(z, 1 - spot.q, p)
            self.arrive(OUTER, far)

            @pl.when(z // 2 == spot.p)
            def _():
                self.arrive(MIX, far)

    def sent(self):
        def act(copy):
            copy.wait_send()

        self.begin_pair(act)
        self.begin(act)
        for t in range(4):
            self.each(t, lambda sign: self.hop(t, sign, act, False))
            self.launch_last(t, act, False)
            if t:
                self.each(t, lambda sign: self.hop_last(t, sign, act, False))


class Edges:
    def __init__(self, spot, level, source, first, buffer, send_sem, recv_sem):
        self.me, self.level, self.source, self.first, self.buffer = spot.me, level, source, first, buffer
        self.send_sem, self.recv_sem = send_sem, recv_sem
        self.rows = buffer.shape[1] - 2 * EDGE
        self.same = level is spot.level
        self.section = level

    def land(self, side, slot):
        return self.buffer.at[slot, pl.ds(0 if side == 0 else EDGE + self.rows, EDGE), :]

    def sends(self, remote, local):
        for side in (0, 1):
            there = self.me < 15 if side == 0 else self.me > 0
            near = self.me + 1 if side == 0 else self.me - 1
            for slot in (0, 1):
                target = near if slot == 0 else mate(near)
                start = self.first + (self.rows - EDGE if side == 0 else 0)
                source = self.source(start)
                copy = pltpu.make_async_remote_copy(
                    src_ref=source,
                    dst_ref=self.land(side, slot),
                    send_sem=self.send_sem.at[side, slot],
                    recv_sem=self.recv_sem.at[side, slot],
                    device_id={"ctx": target, "section": self.section},
                    device_id_type=MESH,
                )
                if slot == 0 or not self.same:
                    pl.when(there)(lambda: remote(copy))
                else:
                    pl.when(there & (target != self.me))(lambda: remote(copy))
                    if local is not None:
                        pl.when(there & (target == self.me))(
                            lambda: local(
                                pltpu.make_async_copy(source, self.land(side, slot), self.recv_sem.at[side, slot])
                            )
                        )

    def start(self):
        self.sends(lambda c: c.start(), lambda c: c.start())

    def sent(self):
        self.sends(lambda c: c.wait_send(), None)

    def receive(self):
        for slot in (0, 1):
            block = self.me if slot == 0 else mate(self.me)
            for side in (0, 1):
                there = block > 0 if side == 0 else block < 15
                giver = block - 1 if side == 0 else block + 1
                land = self.land(side, slot)
                source = self.buffer.at[0, pl.ds(EDGE, EDGE), :]

                arrived = pltpu.make_async_remote_copy(
                    src_ref=source,
                    dst_ref=land,
                    send_sem=self.send_sem.at[side, slot],
                    recv_sem=self.recv_sem.at[side, slot],
                    device_id={"ctx": giver, "section": 1},
                    device_id_type=MESH,
                )
                if self.same:
                    pl.when(there & (giver != self.me))(arrived.wait_recv)
                    pl.when(there & (giver == self.me))(
                        pltpu.make_async_copy(source, land, self.recv_sem.at[side, slot]).wait
                    )
                else:
                    pl.when(there)(arrived.wait_recv)

                @pl.when(jnp.logical_not(there))
                def _():
                    land[...] = jnp.zeros(land.shape, land.dtype)


def columns(count, width, body):
    def step(n, c):
        body(pl.ds(pl.multiple_of(n * width, width), width), n)
        return c

    lax.fori_loop(0, count, step, 0)


def across(left, right):
    return lax.dot_general(left, right, (((1,), (1,)), ((), ())), preferred_element_type=jnp.float32)


def tower_kernel(
    conv_w, mix_w, inputs, scale_in, shift_in, cotangent, out,
    conv_full, mix_full, other, held, scale, shift, factor, hidden, grad, conv_sum, back, dpadded, dconv, dtotal, part_out, part_in, result,
    send_sem, recv_sem, own_sem, load_sem, hid_send, hid_recv, edge_send, edge_recv, cot_send, cot_recv, cedge_send, cedge_recv,
    grad_send, grad_recv, gedge_send, gedge_recv, part_send, part_recv, out_sem, gates,
):
    spot = Spot()
    level, me = spot.level, spot.me
    rows, wide = cotangent.shape
    half = conv_full.shape[1] // 3
    plane = wide // 4
    tall = rows + 2 * EDGE
    tiles = wide // TILE
    middle = pl.ds(EDGE, rows)
    partner = spot.ctx(spot.z, spot.q, 1 - spot.p)
    gather = Gather(spot, conv_w, mix_w, conv_full, mix_full, other, send_sem, recv_sem, own_sem)

    def start(copy):
        copy.start()

    loads = [
        pltpu.make_async_copy(inputs.at[0], held, load_sem.at[0]),
        pltpu.make_async_copy(scale_in, scale, load_sem.at[2]),
        pltpu.make_async_copy(shift_in, shift, load_sem.at[3]),
    ]
    own = gather.own()
    for copy in own + loads:
        copy.start()
    gather.own_mix(start)
    load_cot = pltpu.make_async_copy(cotangent, grad.at[0, middle, :], load_sem.at[1])
    pl.when(level == 1)(load_cot.start)
    greet(spot)
    for copy in own:
        copy.wait()

    def cot_copy():
        return pltpu.make_async_remote_copy(
            src_ref=cotangent, dst_ref=grad.at[1, middle, :], send_sem=cot_send, recv_sem=cot_recv,
            device_id={"ctx": partner}, device_id_type=MESH,
        )

    cot_edges = Edges(spot, level, lambda r: cotangent.at[pl.ds(r, EDGE), :], 0, grad, cedge_send, cedge_recv)

    ends = (spot.z == 0) | (spot.z == 3)

    @pl.when(level == 1)
    def _():
        gather.begin(start)
        gather.begin_pair(start)

    for copy in loads:
        copy.wait()

    def front(cols, _):
        gain = scale[:, cols]
        pre = held[:, cols].astype(jnp.float32) * gain + shift[:, cols]
        act, slope = gelu_parts(pre)
        hidden[0, middle, cols] = act.astype(jnp.bfloat16)
        factor[:, cols] = slope * gain

    columns(wide // LANES, LANES, front)

    def hid_copy():
        return pltpu.make_async_remote_copy(
            src_ref=hidden.at[0, middle, :], dst_ref=hidden.at[1, middle, :], send_sem=hid_send, recv_sem=hid_recv,
            device_id={"ctx": partner}, device_id_type=MESH,
        )

    edges = Edges(spot, level, lambda r: hidden.at[0, pl.ds(r, EDGE), :], EDGE, hidden, edge_send, edge_recv)

    def pair_part():
        pl.semaphore_wait(gates.at[0], 1)
        gather.begin_pair(start)
        hid_copy().start()
        edges.start()

    def rest_part():
        pl.semaphore_wait(gates.at[1], 1)
        gather.begin(start)

    @pl.when(level == 1)
    def _():
        hid_copy().start()
        edges.start()
        cot_copy().start()
        cot_edges.start()

    gather.own_mix(lambda c: c.wait())

    @pl.when((level == 0) & ends)
    def _():
        rest_part()
        pair_part()

    @pl.when((level == 0) & jnp.logical_not(ends))
    def _():
        pair_part()
        rest_part()

    def add_half(here):
        for k in range(2):
            gather.rest(2 * here + k)
        off = pl.ds(pl.multiple_of(2 * here * plane, 2 * plane), 2 * plane)
        near = here is mine

        def slot(n, c):
            term = jnp.dot(hidden[n, :, off], conv_full[off, :], preferred_element_type=jnp.float32)
            if near:
                conv_sum[n] = term
            else:
                conv_sum[n] += term
            return c

        lax.fori_loop(0, 2, slot, 0)

    mine = spot.z // 2

    def grad_copy(n, slot):
        cols = pl.ds(n * TILE, TILE)
        return pltpu.make_async_remote_copy(
            src_ref=result.at[:, cols],
            dst_ref=grad.at[slot, middle, cols],
            send_sem=grad_send.at[n, slot],
            recv_sem=grad_recv.at[n, slot],
            device_id={"ctx": me if slot == 0 else mate(me), "section": 0},
            device_id_type=MESH,
        )

    grad_edges = Edges(spot, 0, lambda r: result.at[pl.ds(r, EDGE), :], 0, grad, gedge_send, gedge_recv)

    def pull(n, c):
        back[n] = across(grad[n], mix_full[...])
        return c

    def open_gates(stage):
        for gate, place in ((0, "pair"), (1, "ends"), (1, "inner")):
            if stage == GATES[place]:
                who = {"pair": True, "ends": ends, "inner": jnp.logical_not(ends)}[place]

                @pl.when((level == 1) & who)
                def _():
                    pl.semaphore_signal(gates.at[gate], inc=1, device_id={"section": 0}, device_id_type=MESH)

    for t in range(4):
        gather.each(t, lambda sign: gather.hop(t, sign, start, True))
        if t == 0:
            gather.side_last()
        gather.launch_last(t, start, True)
        open_gates(t)

    for t in (1, 2):
        gather.each(t, lambda sign: gather.hop_last(t, sign, start, True))
        open_gates(3 + t)

    hid_copy().wait_recv()
    edges.receive()
    add_half(mine)
    open_gates(6)

    @pl.when(level == 1)
    def _():
        load_cot.wait()
        cot_copy().wait_recv()
        cot_edges.receive()

    gather.each(3, lambda sign: gather.hop_last(3, sign, start, True))
    add_half(1 - mine)
    @pl.when(level == 1)
    def _():
        lax.fori_loop(0, 2, pull, 0)

    @pl.when(level == 0)
    def _():
        for n in range(tiles):
            for slot in (0, 1):
                grad_copy(n, slot).wait_recv()
        grad_edges.receive()
        lax.fori_loop(0, 2, pull, 0)

    low, count = EDGE // 2, rows + EDGE

    def slopes(m):
        cols, c0, c1, c2 = (pl.ds(m * LANES + k * half, LANES) for k in (0, 0, 1, 2))
        for n in range(2):
            near = conv_sum[n, low - 1:low - 1 + count, c0] + conv_sum[n, low + 1:low + 1 + count, c2]
            far = conv_sum[n, low - 2:low - 2 + count, c0] + conv_sum[n, low + 2:low + 2 + count, c2]
            conv = jnp.where(level == 0, near, far) + conv_sum[n, low:low + count, c1]
            value = back[n, low:low + count, cols] * gelu_parts(conv)[1]
            dpadded[n, low:low + count, cols] = value.astype(jnp.bfloat16).astype(jnp.float32)
            there = pl.ds(n * rows, rows)
            dconv[there, c1] = dpadded[n, EDGE:EDGE + rows, cols].astype(jnp.bfloat16)
            near = dpadded[n, EDGE + 1:EDGE + 1 + rows, cols]
            far = dpadded[n, EDGE + 2:EDGE + 2 + rows, cols]
            dconv[there, c0] = jnp.where(level == 0, near, far).astype(jnp.bfloat16)
            near = dpadded[n, EDGE - 1:EDGE - 1 + rows, cols]
            far = dpadded[n, EDGE - 2:EDGE - 2 + rows, cols]
            dconv[there, c2] = jnp.where(level == 0, near, far).astype(jnp.bfloat16)

    for m in range(half // LANES):
        slopes(m)

    def part_copy(n):
        return pltpu.make_async_remote_copy(
            src_ref=part_out.at[n], dst_ref=part_in.at[n], send_sem=part_send.at[n], recv_sem=part_recv.at[n],
            device_id={"ctx": partner}, device_id_type=MESH,
        )

    def out_copy(n):
        cols = pl.ds(n * TILE, TILE)
        return pltpu.make_async_copy(result.at[:, cols], out.at[0, :, cols], out_sem.at[n])

    for n in range(tiles + BEHIND):
        if n < tiles:
            cols = pl.ds(n * TILE, TILE)
            term = across(dconv[...], conv_full[cols, :])
            part_out[n] = term[rows:].astype(jnp.bfloat16)
            dtotal[:, cols] = term[:rows]
            part_copy(n).start()
        m = n - BEHIND
        if m >= 0:
            cols = pl.ds(m * TILE, TILE)
            part_copy(m).wait_recv()
            dhidden = dtotal[:, cols] + part_in[m].astype(jnp.float32)
            result[:, cols] = (
                grad[0, middle, cols].astype(jnp.float32) + dhidden * factor[:, cols]
            ).astype(jnp.bfloat16)
            out_copy(m).start()

            @pl.when(level == 1)
            def _():
                grad_copy(m, 0).start()
                grad_copy(m, 1).start()

    @pl.when(level == 1)
    def _():
        grad_edges.start()
        cot_copy().wait_send()
        cot_edges.sent()

    hid_copy().wait_send()
    edges.sent()
    gather.sent()
    for n in range(tiles):
        part_copy(n).wait_send()
        out_copy(n).wait()

    @pl.when(level == 1)
    def _():
        for n in range(tiles):
            for slot in (0, 1):
                grad_copy(n, slot).wait_send()
        grad_edges.sent()


def tower(layer_inputs, conv_weight, mix_weight, bn_scale, bn_shift, cotangent):
    rows, wide = cotangent.shape
    inner = conv_weight.shape[3]
    half = inner // 2
    tall = rows + 2 * EDGE
    tiles = wide // TILE
    anywhere = pl.BlockSpec(memory_space=pl.ANY)
    bf16, f32 = jnp.bfloat16, jnp.float32
    dma = pltpu.SemaphoreType.DMA
    return pl.pallas_call(
        tower_kernel,
        out_shape=jax.ShapeDtypeStruct(layer_inputs.shape, bf16),
        in_specs=[anywhere] * 6,
        out_specs=anywhere,
        scratch_shapes=[
            pltpu.VMEM((wide, 3 * half), bf16),
            pltpu.VMEM((half, wide), bf16),
            pltpu.VMEM((conv_weight.shape[2], 3 * half), bf16),
            pltpu.VMEM((rows, wide), bf16),
            pltpu.VMEM((1, wide), f32),
            pltpu.VMEM((1, wide), f32),
            pltpu.VMEM((rows, wide), f32),
            pltpu.VMEM((2, tall, wide), bf16),
            pltpu.VMEM((2, tall, wide), bf16),
            pltpu.VMEM((2, tall, 3 * half), f32),
            pltpu.VMEM((2, tall, half), f32),
            pltpu.VMEM((2, tall, half), f32),
            pltpu.VMEM((2 * rows, 3 * half), bf16),
            pltpu.VMEM((rows, wide), f32),
            pltpu.VMEM((tiles, rows, TILE), bf16),
            pltpu.VMEM((tiles, rows, TILE), bf16),
            pltpu.VMEM((rows, wide), bf16),
            dma((3, 16, 4)),
            dma((3, 16)),
            dma((4, 2)),
            dma((4,)),
            dma,
            dma,
            dma((2, 2)),
            dma((2, 2)),
            dma,
            dma,
            dma((2, 2)),
            dma((2, 2)),
            dma((tiles, 2)),
            dma((tiles, 2)),
            dma((2, 2)),
            dma((2, 2)),
            dma((tiles,)),
            dma((tiles,)),
            dma((tiles,)),
            pltpu.SemaphoreType.REGULAR((2,)),
        ],
        compiler_params=pltpu.CompilerParams(
            collective_id=0, has_side_effects=True, vmem_limit_bytes=64 * 1024 * 1024
        ),
    )(conv_weight, mix_weight, layer_inputs, bn_scale, bn_shift, cotangent)


def extended(cells, sides, width):
    for axis, dim in sides:
        count = lax.axis_size(axis)
        ends = count - 1
        head = lax.slice_in_dim(cells, 0, width, axis=dim)
        tail = lax.slice_in_dim(cells, cells.shape[dim] - width, cells.shape[dim], axis=dim)
        cells = jnp.concatenate(
            [
                lax.ppermute(tail, axis, [(i, (i + 1) % count) for i in range(ends)]),
                cells,
                lax.ppermute(head, axis, [((i + 1) % count, i) for i in range(ends)]),
            ],
            axis=dim,
        )
    return cells


def shifted(block, axis, distance):
    devices = range(lax.axis_size(axis))
    route = [(i - distance, i) for i in devices if i - distance in devices]
    return lax.ppermute(block, axis, route)


def gelu_parts(value):
    cdf = 0.5 * (1.0 + lax.erf(value * 0.7071067811865476))
    dens = jnp.exp(-0.5 * value * value) * 0.3989422804014327
    return (value * cdf, cdf + value * dens)


def shards(layer_inputs, conv_weight, mix_weight, bn_scale, bn_shift, cotangent):
    sections = lax.axis_size("section")
    level = lax.axis_index("section")
    widest = 2 ** (sections - 1)
    if lax.axis_size("ctx") == 16 and sections == 2:
        return tower(layer_inputs, conv_weight, mix_weight, bn_scale, bn_shift, cotangent)
    conv_full = lax.all_gather(conv_weight, "ctx", axis=2, tiled=True)[0]
    mix_full = lax.all_gather(mix_weight, "ctx", axis=1, tiled=True)[0]
    rows = cotangent.shape[0]
    inner = mix_full.shape[0]
    spacing = jnp.left_shift(jnp.int32(1), level)
    pre = layer_inputs[0].astype(jnp.float32) * bn_scale[0] + bn_shift[0]
    act, slope_pre = gelu_parts(pre)
    hidden = act.astype(jnp.bfloat16)
    padded = extended(hidden, (("ctx", 0),), widest)
    conv = jnp.zeros((rows, inner), jnp.float32)
    for k in range(3):
        window = lax.dynamic_slice_in_dim(padded, widest + (k - 1) * spacing, rows, 0)
        conv = conv + jnp.dot(window, conv_full[k], preferred_element_type=jnp.float32)
    _, slope_conv = gelu_parts(conv)
    factor = slope_pre * bn_scale[0]

    def make_dconv(grad):
        back = jnp.einsum("pc,hc->ph", grad, mix_full, preferred_element_type=jnp.float32)
        return (back * slope_conv).astype(jnp.bfloat16)

    def skip_dconv(grad):
        return jnp.zeros((rows, inner), jnp.bfloat16)

    def finish(grad, dpad, starts):
        dhidden = jnp.zeros((rows, conv_full.shape[1]), jnp.float32)
        for k in range(3):
            window = lax.dynamic_slice_in_dim(dpad, starts[k], rows, 0)
            dhidden = dhidden + jnp.einsum(
                "ph,ch->pc", window, conv_full[k], preferred_element_type=jnp.float32
            )
        return (grad.astype(jnp.float32) + dhidden * factor).astype(jnp.bfloat16)

    mine = jnp.zeros_like(cotangent)

    def turn(step, carry):
        grad, mine = carry
        active = level == sections - 1 - step
        dconv = lax.cond(active, make_dconv, skip_dconv, grad)
        dpad = extended(dconv, (("ctx", 0),), widest)
        starts = [widest + (1 - k) * spacing for k in range(3)]
        result = lax.cond(active, lambda g: finish(g, dpad, starts), lambda g: g, grad)
        mine = jnp.where(active, result, mine)
        grad = shifted(result, "section", -1)
        return (grad, mine)

    grad, mine = lax.fori_loop(0, sections, turn, (cotangent, mine))
    return mine[None]


def solution(mesh):
    return jax.shard_map(
        shards,
        mesh=mesh,
        in_specs=(
            P("section", "ctx", None),
            P("section", None, "ctx", None),
            P("section", "ctx", None),
            P("section", None),
            P("section", None),
            P("ctx", None),
        ),
        out_specs=P("section", "ctx", None),
        check_vma=False,
    )
```

```python
import jax
import jax.numpy as jnp
from jax import lax
from jax.experimental import pallas as pl
from jax.experimental.pallas import tpu as pltpu
from jax.sharding import PartitionSpec as P

MESH = pl.DeviceIdType.MESH
EDGE = 16
LANES = 128
TILE = 256
DEVICES = 32
GATES = {"pair": 3, "ends": 1, "inner": 5}
BEHIND = 3


def mate(c):
    return c + 1 - 2 * (c % 2)


class Spot:
    def __init__(self):
        self.level = lax.axis_index("section")
        self.me = me = lax.axis_index("ctx")
        self.z, self.q, self.p = me // 4, (me // 2) % 2, me % 2

    def ctx(self, z, q, p):
        return z * 4 + q * 2 + p


def greet(spot):
    barrier = pltpu.get_barrier_semaphore()
    index = spot.me * 2 + spot.level

    def hello(k, c):
        device = (index + k) % DEVICES
        pl.semaphore_signal(
            barrier, inc=1, device_id={"ctx": device // 2, "section": device % 2}, device_id_type=MESH
        )
        return c

    lax.fori_loop(1, DEVICES, hello, 0)
    pl.semaphore_wait(barrier, DEVICES - 1)


PAIR, SIDE, UP, DOWN = range(4)
OUTER, LAST, MIX = range(3)


class Gather:
    def __init__(self, spot, conv, mix, conv_full, mix_full, other, send_sem, recv_sem, own_sem):
        self.spot, self.conv, self.mix, self.conv_full, self.mix_full = spot, conv, mix, conv_full, mix_full
        self.other, self.send_sem, self.recv_sem, self.own_sem = other, send_sem, recv_sem, own_sem
        self.depth, self.inner = conv.shape[2], mix.shape[1]
        self.half = conv_full.shape[1] // 3

    def taps(self, kind):
        return pl.ds(0, 2 * self.half) if kind == OUTER else pl.ds(2 * self.half, self.half)

    def full(self, kind, source):
        if kind != MIX:
            rows = pl.ds(pl.multiple_of(source * self.depth, 16), self.depth)
            return self.conv_full.at[rows, self.taps(kind)]
        return self.mix_full.at[pl.ds(pl.multiple_of((source % 8) * self.inner, 16), self.inner), :]

    def copy(self, kind, source, mine, lane):
        spot = self.spot
        z, q, p = spot.z, spot.q, spot.p
        device = (
            spot.ctx(z, q, 1 - p), spot.ctx(z, 1 - q, p), spot.ctx(z + 1, q, p), spot.ctx(z - 1, q, p),
        )[lane]
        here = self.full(kind, source)
        if mine and kind == MIX:
            here = self.mix.at[0]
        elif mine and lane == PAIR:
            here = self.other.at[:, self.taps(kind)]
        return pltpu.make_async_remote_copy(
            src_ref=here,
            dst_ref=self.full(kind, source),
            send_sem=self.send_sem.at[kind, source, lane],
            recv_sem=self.recv_sem.at[kind, source],
            device_id={"ctx": device},
            device_id_type=MESH,
        )

    def send(self, kind, source, mine, lane, act):
        z = self.spot.z
        if lane == UP:
            pl.when(z < 3)(lambda: act(self.copy(kind, source, mine, lane)))
        elif lane == DOWN:
            pl.when(z > 0)(lambda: act(self.copy(kind, source, mine, lane)))
        else:
            act(self.copy(kind, source, mine, lane))

    def own(self):
        spot = self.spot
        copies = []
        for k in range(3):
            for n, p in enumerate((spot.p, 1 - spot.p)):
                cols = pl.ds(k * self.half, self.half)
                rows = pl.ds(pl.multiple_of(spot.me * self.depth, 16), self.depth)
                copies.append(
                    pltpu.make_async_copy(
                        self.conv.at[0, k, :, pl.ds(pl.multiple_of(p * self.half, 128), self.half)],
                        self.other.at[:, cols] if n else self.conv_full.at[rows, cols],
                        self.own_sem.at[k, n],
                    )
                )
        return copies

    def own_mix(self, act):
        spot = self.spot
        pl.when(spot.z // 2 == spot.p)(
            lambda: act(pltpu.make_async_copy(self.mix.at[0], self.full(MIX, spot.me), self.own_sem.at[3, 0]))
        )

    def begin_pair(self, act):
        spot = self.spot
        self.send(OUTER, spot.me, True, PAIR, act)

        @pl.when(spot.z // 2 == 1 - spot.p)
        def _():
            self.send(MIX, spot.me, True, PAIR, act)

        self.send(LAST, spot.me, True, PAIR, act)

    def begin(self, act):
        spot = self.spot
        me = spot.me
        for lane in (UP, DOWN):
            self.send(OUTER, me, True, lane, act)
        self.send(LAST, me, True, SIDE, act)

        @pl.when(spot.z // 2 == spot.p)
        def _():
            for lane in (UP, DOWN, SIDE):
                self.send(MIX, me, True, lane, act)

        self.send(OUTER, me, True, SIDE, act)

    def onward(self, kind, source, t, sign, act):
        if t == 0:
            self.send(kind, source, False, UP, act)
            self.send(kind, source, False, DOWN, act)
        else:

            @pl.when(sign < 0)
            def _():
                self.send(kind, source, False, UP, act)

            @pl.when(sign > 0)
            def _():
                self.send(kind, source, False, DOWN, act)

    def arrive(self, kind, source):
        self.copy(kind, source, False, PAIR).wait_recv()

    def each(self, t, body):
        if t == 0:
            body(0)
            return
        z = self.spot.z

        def side(b, c):
            sign = 1 - 2 * b

            @pl.when((z + sign * t >= 0) & (z + sign * t < 4))
            def _():
                body(sign)

            return c

        lax.fori_loop(0, 2, side, 0)

    def hop(self, t, sign, act, wait):
        spot = self.spot
        z, q, p = spot.z + sign * t, spot.q, spot.p
        for dp in (0, 1) if t else (1,):
            near = spot.ctx(z, q, 1 - p if dp else p)
            if wait:
                self.arrive(OUTER, near)
            self.onward(OUTER, near, t, sign, act)
            self.send(OUTER, near, False, SIDE, act)

            @pl.when(z // 2 == p)
            def _():
                if wait:
                    self.arrive(MIX, near)
                self.onward(MIX, near, t, sign, act)
                self.send(MIX, near, False, SIDE, act)

            if t == 0:
                if wait:
                    self.arrive(LAST, near)
                self.send(LAST, near, False, SIDE, act)

    def hop_last(self, t, sign, act, wait):
        spot = self.spot
        z = spot.z + sign * t
        for q in (spot.q, 1 - spot.q):
            for p in (spot.p, 1 - spot.p):
                source = spot.ctx(z, q, p)
                if wait:
                    self.arrive(LAST, source)
                self.onward(LAST, source, t, sign, act)

    def launch_last(self, t, act, wait):
        spot = self.spot
        for lane, ready in ((DOWN, spot.z + t == 3), (UP, spot.z == t)):

            @pl.when(ready)
            def _():
                for q in (0, 1):
                    for p in (0, 1):
                        self.send(LAST, spot.ctx(spot.z, q, p), False, lane, act)

    def side_last(self):
        spot = self.spot
        for p in (0, 1):
            self.arrive(LAST, spot.ctx(spot.z, 1 - spot.q, p))

    def rest(self, z):
        spot = self.spot
        for p in (0, 1):
            far = spot.ctx(z, 1 - spot.q, p)
            self.arrive(OUTER, far)

            @pl.when(z // 2 == spot.p)
            def _():
                self.arrive(MIX, far)

    def sent(self):
        def act(copy):
            copy.wait_send()

        self.begin_pair(act)
        self.begin(act)
        for t in range(4):
            self.each(t, lambda sign: self.hop(t, sign, act, False))
            self.launch_last(t, act, False)
            if t:
                self.each(t, lambda sign: self.hop_last(t, sign, act, False))


class Edges:
    def __init__(self, spot, level, source, first, buffer, send_sem, recv_sem):
        self.me, self.level, self.source, self.first, self.buffer = spot.me, level, source, first, buffer
        self.send_sem, self.recv_sem = send_sem, recv_sem
        self.rows = buffer.shape[1] - 2 * EDGE
        self.same = level is spot.level
        self.section = level

    def land(self, side, slot):
        return self.buffer.at[slot, pl.ds(0 if side == 0 else EDGE + self.rows, EDGE), :]

    def sends(self, remote, local):
        for side in (0, 1):
            there = self.me < 15 if side == 0 else self.me > 0
            near = self.me + 1 if side == 0 else self.me - 1
            for slot in (0, 1):
                target = near if slot == 0 else mate(near)
                start = self.first + (self.rows - EDGE if side == 0 else 0)
                source = self.source(start)
                copy = pltpu.make_async_remote_copy(
                    src_ref=source,
                    dst_ref=self.land(side, slot),
                    send_sem=self.send_sem.at[side, slot],
                    recv_sem=self.recv_sem.at[side, slot],
                    device_id={"ctx": target, "section": self.section},
                    device_id_type=MESH,
                )
                if slot == 0 or not self.same:
                    pl.when(there)(lambda: remote(copy))
                else:
                    pl.when(there & (target != self.me))(lambda: remote(copy))
                    if local is not None:
                        pl.when(there & (target == self.me))(
                            lambda: local(
                                pltpu.make_async_copy(source, self.land(side, slot), self.recv_sem.at[side, slot])
                            )
                        )

    def start(self):
        self.sends(lambda c: c.start(), lambda c: c.start())

    def sent(self):
        self.sends(lambda c: c.wait_send(), None)

    def receive(self):
        for slot in (0, 1):
            block = self.me if slot == 0 else mate(self.me)
            for side in (0, 1):
                there = block > 0 if side == 0 else block < 15
                giver = block - 1 if side == 0 else block + 1
                land = self.land(side, slot)
                source = self.buffer.at[0, pl.ds(EDGE, EDGE), :]

                arrived = pltpu.make_async_remote_copy(
                    src_ref=source,
                    dst_ref=land,
                    send_sem=self.send_sem.at[side, slot],
                    recv_sem=self.recv_sem.at[side, slot],
                    device_id={"ctx": giver, "section": 1},
                    device_id_type=MESH,
                )
                if self.same:
                    pl.when(there & (giver != self.me))(arrived.wait_recv)
                    pl.when(there & (giver == self.me))(
                        pltpu.make_async_copy(source, land, self.recv_sem.at[side, slot]).wait
                    )
                else:
                    pl.when(there)(arrived.wait_recv)

                @pl.when(jnp.logical_not(there))
                def _():
                    land[...] = jnp.zeros(land.shape, land.dtype)


def columns(count, width, body):
    def step(n, c):
        body(pl.ds(pl.multiple_of(n * width, width), width), n)
        return c

    lax.fori_loop(0, count, step, 0)


def across(left, right):
    return lax.dot_general(left, right, (((1,), (1,)), ((), ())), preferred_element_type=jnp.float32)


def tower_kernel(
    conv_w, mix_w, inputs, scale_in, shift_in, cotangent, out,
    conv_full, mix_full, other, held, scale, shift, factor, hidden, grad, conv_sum, back, dpadded, dconv, dtotal, part_out, part_in, result,
    send_sem, recv_sem, own_sem, load_sem, hid_send, hid_recv, edge_send, edge_recv, cot_send, cot_recv, cedge_send, cedge_recv,
    grad_send, grad_recv, gedge_send, gedge_recv, part_send, part_recv, out_sem, gates,
):
    spot = Spot()
    level, me = spot.level, spot.me
    rows, wide = cotangent.shape
    half = conv_full.shape[1] // 3
    plane = wide // 4
    tall = rows + 2 * EDGE
    tiles = wide // TILE
    middle = pl.ds(EDGE, rows)
    partner = spot.ctx(spot.z, spot.q, 1 - spot.p)
    gather = Gather(spot, conv_w, mix_w, conv_full, mix_full, other, send_sem, recv_sem, own_sem)

    def start(copy):
        copy.start()

    loads = [
        pltpu.make_async_copy(inputs.at[0], held, load_sem.at[0]),
        pltpu.make_async_copy(scale_in, scale, load_sem.at[2]),
        pltpu.make_async_copy(shift_in, shift, load_sem.at[3]),
    ]
    own = gather.own()
    for copy in own + loads:
        copy.start()
    gather.own_mix(start)
    load_cot = pltpu.make_async_copy(cotangent, grad.at[0, middle, :], load_sem.at[1])
    pl.when(level == 1)(load_cot.start)
    greet(spot)
    for copy in own:
        copy.wait()

    def cot_copy():
        return pltpu.make_async_remote_copy(
            src_ref=cotangent, dst_ref=grad.at[1, middle, :], send_sem=cot_send, recv_sem=cot_recv,
            device_id={"ctx": partner}, device_id_type=MESH,
        )

    cot_edges = Edges(spot, level, lambda r: cotangent.at[pl.ds(r, EDGE), :], 0, grad, cedge_send, cedge_recv)

    ends = (spot.z == 0) | (spot.z == 3)

    @pl.when(level == 1)
    def _():
        gather.begin(start)
        gather.begin_pair(start)

    for copy in loads:
        copy.wait()

    def front(cols, _):
        gain = scale[:, cols]
        pre = held[:, cols].astype(jnp.float32) * gain + shift[:, cols]
        act, slope = gelu_parts(pre)
        hidden[0, middle, cols] = act.astype(jnp.bfloat16)
        factor[:, cols] = slope * gain

    columns(wide // LANES, LANES, front)

    def hid_copy():
        return pltpu.make_async_remote_copy(
            src_ref=hidden.at[0, middle, :], dst_ref=hidden.at[1, middle, :], send_sem=hid_send, recv_sem=hid_recv,
            device_id={"ctx": partner}, device_id_type=MESH,
        )

    edges = Edges(spot, level, lambda r: hidden.at[0, pl.ds(r, EDGE), :], EDGE, hidden, edge_send, edge_recv)

    def pair_part():
        pl.semaphore_wait(gates.at[0], 1)
        gather.begin_pair(start)
        hid_copy().start()
        edges.start()

    def rest_part():
        pl.semaphore_wait(gates.at[1], 1)
        gather.begin(start)

    @pl.when(level == 1)
    def _():
        hid_copy().start()
        edges.start()
        cot_copy().start()
        cot_edges.start()

    gather.own_mix(lambda c: c.wait())

    @pl.when((level == 0) & ends)
    def _():
        rest_part()
        pair_part()

    @pl.when((level == 0) & jnp.logical_not(ends))
    def _():
        pair_part()
        rest_part()

    def add_half(here, cols):
        off = pl.ds(pl.multiple_of(2 * here * plane, 2 * plane), 2 * plane)
        near = here is mine

        def slot(n, c):
            term = jnp.dot(hidden[n, :, off], conv_full[off, cols], preferred_element_type=jnp.float32)
            if near:
                conv_sum[n, :, cols] = term
            else:
                conv_sum[n, :, cols] += term
            return c

        lax.fori_loop(0, 2, slot, 0)

    mine = spot.z // 2

    def grad_copy(n, slot):
        cols = pl.ds(n * TILE, TILE)
        return pltpu.make_async_remote_copy(
            src_ref=result.at[:, cols],
            dst_ref=grad.at[slot, middle, cols],
            send_sem=grad_send.at[n, slot],
            recv_sem=grad_recv.at[n, slot],
            device_id={"ctx": me if slot == 0 else mate(me), "section": 0},
            device_id_type=MESH,
        )

    grad_edges = Edges(spot, 0, lambda r: result.at[pl.ds(r, EDGE), :], 0, grad, gedge_send, gedge_recv)

    def pull(n, c):
        back[n] = across(grad[n], mix_full[...])
        return c

    def open_gates(stage):
        for gate, place in ((0, "pair"), (1, "ends"), (1, "inner")):
            if stage == GATES[place]:
                who = {"pair": True, "ends": ends, "inner": jnp.logical_not(ends)}[place]

                @pl.when((level == 1) & who)
                def _():
                    pl.semaphore_signal(gates.at[gate], inc=1, device_id={"section": 0}, device_id_type=MESH)

    for t in range(4):
        gather.each(t, lambda sign: gather.hop(t, sign, start, True))
        if t == 0:
            gather.side_last()
        gather.launch_last(t, start, True)
        open_gates(t)

    for t in (1, 2):
        gather.each(t, lambda sign: gather.hop_last(t, sign, start, True))
        open_gates(3 + t)

    hid_copy().wait_recv()
    edges.receive()
    for k in range(2):
        gather.rest(2 * mine + k)
    add_half(mine, pl.ds(0, 3 * half))
    open_gates(6)
    for k in range(2):
        gather.rest(2 * (1 - mine) + k)
    add_half(1 - mine, gather.taps(OUTER))

    @pl.when(level == 1)
    def _():
        load_cot.wait()
        cot_copy().wait_recv()
        cot_edges.receive()

    @pl.when(level == 0)
    def _():
        for n in range(tiles):
            for slot in (0, 1):
                grad_copy(n, slot).wait_recv()
        grad_edges.receive()

    lax.fori_loop(0, 2, pull, 0)
    gather.each(3, lambda sign: gather.hop_last(3, sign, start, True))
    add_half(1 - mine, gather.taps(LAST))

    low, count = EDGE // 2, rows + EDGE

    def slopes(m):
        cols, c0, c1, c2 = (pl.ds(m * LANES + k * half, LANES) for k in (0, 0, 1, 2))
        for n in range(2):
            near = conv_sum[n, low - 1:low - 1 + count, c0] + conv_sum[n, low + 1:low + 1 + count, c2]
            far = conv_sum[n, low - 2:low - 2 + count, c0] + conv_sum[n, low + 2:low + 2 + count, c2]
            conv = jnp.where(level == 0, near, far) + conv_sum[n, low:low + count, c1]
            value = back[n, low:low + count, cols] * gelu_parts(conv)[1]
            dpadded[n, low:low + count, cols] = value.astype(jnp.bfloat16).astype(jnp.float32)
            there = pl.ds(n * rows, rows)
            dconv[there, c1] = dpadded[n, EDGE:EDGE + rows, cols].astype(jnp.bfloat16)
            near = dpadded[n, EDGE + 1:EDGE + 1 + rows, cols]
            far = dpadded[n, EDGE + 2:EDGE + 2 + rows, cols]
            dconv[there, c0] = jnp.where(level == 0, near, far).astype(jnp.bfloat16)
            near = dpadded[n, EDGE - 1:EDGE - 1 + rows, cols]
            far = dpadded[n, EDGE - 2:EDGE - 2 + rows, cols]
            dconv[there, c2] = jnp.where(level == 0, near, far).astype(jnp.bfloat16)

    for m in range(half // LANES):
        slopes(m)

    def part_copy(n):
        return pltpu.make_async_remote_copy(
            src_ref=part_out.at[n], dst_ref=part_in.at[n], send_sem=part_send.at[n], recv_sem=part_recv.at[n],
            device_id={"ctx": partner}, device_id_type=MESH,
        )

    def out_copy(n):
        cols = pl.ds(n * TILE, TILE)
        return pltpu.make_async_copy(result.at[:, cols], out.at[0, :, cols], out_sem.at[n])

    def settle():
        hid_copy().wait_send()
        edges.sent()
        gather.sent()

        @pl.when(level == 1)
        def _():
            cot_copy().wait_send()
            cot_edges.sent()

    for n in range(tiles + BEHIND):
        if n < tiles:
            cols = pl.ds(n * TILE, TILE)
            term = across(dconv[...], conv_full[cols, :])
            part_out[n] = term[rows:].astype(jnp.bfloat16)
            dtotal[:, cols] = term[:rows]
            part_copy(n).start()
        if n == tiles - 1:
            settle()
        m = n - BEHIND
        if m >= 0:
            cols = pl.ds(m * TILE, TILE)
            part_copy(m).wait_recv()
            dhidden = dtotal[:, cols] + part_in[m].astype(jnp.float32)
            result[:, cols] = (
                grad[0, middle, cols].astype(jnp.float32) + dhidden * factor[:, cols]
            ).astype(jnp.bfloat16)
            out_copy(m).start()

            @pl.when(level == 1)
            def _():
                grad_copy(m, 0).start()
                grad_copy(m, 1).start()

    @pl.when(level == 1)
    def _():
        grad_edges.start()
    for n in range(tiles):
        part_copy(n).wait_send()
        out_copy(n).wait()

    @pl.when(level == 1)
    def _():
        for n in range(tiles):
            for slot in (0, 1):
                grad_copy(n, slot).wait_send()
        grad_edges.sent()


def tower(layer_inputs, conv_weight, mix_weight, bn_scale, bn_shift, cotangent):
    rows, wide = cotangent.shape
    inner = conv_weight.shape[3]
    half = inner // 2
    tall = rows + 2 * EDGE
    tiles = wide // TILE
    anywhere = pl.BlockSpec(memory_space=pl.ANY)
    bf16, f32 = jnp.bfloat16, jnp.float32
    dma = pltpu.SemaphoreType.DMA
    return pl.pallas_call(
        tower_kernel,
        out_shape=jax.ShapeDtypeStruct(layer_inputs.shape, bf16),
        in_specs=[anywhere] * 6,
        out_specs=anywhere,
        scratch_shapes=[
            pltpu.VMEM((wide, 3 * half), bf16),
            pltpu.VMEM((half, wide), bf16),
            pltpu.VMEM((conv_weight.shape[2], 3 * half), bf16),
            pltpu.VMEM((rows, wide), bf16),
            pltpu.VMEM((1, wide), f32),
            pltpu.VMEM((1, wide), f32),
            pltpu.VMEM((rows, wide), f32),
            pltpu.VMEM((2, tall, wide), bf16),
            pltpu.VMEM((2, tall, wide), bf16),
            pltpu.VMEM((2, tall, 3 * half), f32),
            pltpu.VMEM((2, tall, half), f32),
            pltpu.VMEM((2, tall, half), f32),
            pltpu.VMEM((2 * rows, 3 * half), bf16),
            pltpu.VMEM((rows, wide), f32),
            pltpu.VMEM((tiles, rows, TILE), bf16),
            pltpu.VMEM((tiles, rows, TILE), bf16),
            pltpu.VMEM((rows, wide), bf16),
            dma((3, 16, 4)),
            dma((3, 16)),
            dma((4, 2)),
            dma((4,)),
            dma,
            dma,
            dma((2, 2)),
            dma((2, 2)),
            dma,
            dma,
            dma((2, 2)),
            dma((2, 2)),
            dma((tiles, 2)),
            dma((tiles, 2)),
            dma((2, 2)),
            dma((2, 2)),
            dma((tiles,)),
            dma((tiles,)),
            dma((tiles,)),
            pltpu.SemaphoreType.REGULAR((2,)),
        ],
        compiler_params=pltpu.CompilerParams(
            collective_id=0, has_side_effects=True, vmem_limit_bytes=64 * 1024 * 1024
        ),
    )(conv_weight, mix_weight, layer_inputs, bn_scale, bn_shift, cotangent)


def extended(cells, sides, width):
    for axis, dim in sides:
        count = lax.axis_size(axis)
        ends = count - 1
        head = lax.slice_in_dim(cells, 0, width, axis=dim)
        tail = lax.slice_in_dim(cells, cells.shape[dim] - width, cells.shape[dim], axis=dim)
        cells = jnp.concatenate(
            [
                lax.ppermute(tail, axis, [(i, (i + 1) % count) for i in range(ends)]),
                cells,
                lax.ppermute(head, axis, [((i + 1) % count, i) for i in range(ends)]),
            ],
            axis=dim,
        )
    return cells


def shifted(block, axis, distance):
    devices = range(lax.axis_size(axis))
    route = [(i - distance, i) for i in devices if i - distance in devices]
    return lax.ppermute(block, axis, route)


def gelu_parts(value):
    cdf = 0.5 * (1.0 + lax.erf(value * 0.7071067811865476))
    dens = jnp.exp(-0.5 * value * value) * 0.3989422804014327
    return (value * cdf, cdf + value * dens)


def shards(layer_inputs, conv_weight, mix_weight, bn_scale, bn_shift, cotangent):
    sections = lax.axis_size("section")
    level = lax.axis_index("section")
    widest = 2 ** (sections - 1)
    if lax.axis_size("ctx") == 16 and sections == 2:
        return tower(layer_inputs, conv_weight, mix_weight, bn_scale, bn_shift, cotangent)
    conv_full = lax.all_gather(conv_weight, "ctx", axis=2, tiled=True)[0]
    mix_full = lax.all_gather(mix_weight, "ctx", axis=1, tiled=True)[0]
    rows = cotangent.shape[0]
    inner = mix_full.shape[0]
    spacing = jnp.left_shift(jnp.int32(1), level)
    pre = layer_inputs[0].astype(jnp.float32) * bn_scale[0] + bn_shift[0]
    act, slope_pre = gelu_parts(pre)
    hidden = act.astype(jnp.bfloat16)
    padded = extended(hidden, (("ctx", 0),), widest)
    conv = jnp.zeros((rows, inner), jnp.float32)
    for k in range(3):
        window = lax.dynamic_slice_in_dim(padded, widest + (k - 1) * spacing, rows, 0)
        conv = conv + jnp.dot(window, conv_full[k], preferred_element_type=jnp.float32)
    _, slope_conv = gelu_parts(conv)
    factor = slope_pre * bn_scale[0]

    def make_dconv(grad):
        back = jnp.einsum("pc,hc->ph", grad, mix_full, preferred_element_type=jnp.float32)
        return (back * slope_conv).astype(jnp.bfloat16)

    def skip_dconv(grad):
        return jnp.zeros((rows, inner), jnp.bfloat16)

    def finish(grad, dpad, starts):
        dhidden = jnp.zeros((rows, conv_full.shape[1]), jnp.float32)
        for k in range(3):
            window = lax.dynamic_slice_in_dim(dpad, starts[k], rows, 0)
            dhidden = dhidden + jnp.einsum(
                "ph,ch->pc", window, conv_full[k], preferred_element_type=jnp.float32
            )
        return (grad.astype(jnp.float32) + dhidden * factor).astype(jnp.bfloat16)

    mine = jnp.zeros_like(cotangent)

    def turn(step, carry):
        grad, mine = carry
        active = level == sections - 1 - step
        dconv = lax.cond(active, make_dconv, skip_dconv, grad)
        dpad = extended(dconv, (("ctx", 0),), widest)
        starts = [widest + (1 - k) * spacing for k in range(3)]
        result = lax.cond(active, lambda g: finish(g, dpad, starts), lambda g: g, grad)
        mine = jnp.where(active, result, mine)
        grad = shifted(result, "section", -1)
        return (grad, mine)

    grad, mine = lax.fori_loop(0, sections, turn, (cotangent, mine))
    return mine[None]


def solution(mesh):
    return jax.shard_map(
        shards,
        mesh=mesh,
        in_specs=(
            P("section", "ctx", None),
            P("section", None, "ctx", None),
            P("section", "ctx", None),
            P("section", None),
            P("section", None),
            P("ctx", None),
        ),
        out_specs=P("section", "ctx", None),
        check_vma=False,
    )
```

```python
import jax
import jax.numpy as jnp
from jax import lax
from jax.experimental import pallas as pl
from jax.experimental.pallas import tpu as pltpu
from jax.sharding import PartitionSpec as P

MESH = pl.DeviceIdType.MESH
EDGE = 16
LANES = 128
TILE = 256
DEVICES = 32
GATES = {"pair": 3, "ends": 1, "inner": 5}
BEHIND = 4


def mate(c):
    return c + 1 - 2 * (c % 2)


class Spot:
    def __init__(self):
        self.level = lax.axis_index("section")
        self.me = me = lax.axis_index("ctx")
        self.z, self.q, self.p = me // 4, (me // 2) % 2, me % 2

    def ctx(self, z, q, p):
        return z * 4 + q * 2 + p


def greet(spot):
    barrier = pltpu.get_barrier_semaphore()
    index = spot.me * 2 + spot.level

    def hello(k, c):
        device = (index + k) % DEVICES
        pl.semaphore_signal(
            barrier, inc=1, device_id={"ctx": device // 2, "section": device % 2}, device_id_type=MESH
        )
        return c

    lax.fori_loop(1, DEVICES, hello, 0)
    pl.semaphore_wait(barrier, DEVICES - 1)


PAIR, SIDE, UP, DOWN = range(4)
OUTER, LAST, MIX = range(3)


class Gather:
    def __init__(self, spot, conv, mix, conv_full, mix_full, other, send_sem, recv_sem, own_sem):
        self.spot, self.conv, self.mix, self.conv_full, self.mix_full = spot, conv, mix, conv_full, mix_full
        self.other, self.send_sem, self.recv_sem, self.own_sem = other, send_sem, recv_sem, own_sem
        self.depth, self.inner = conv.shape[2], mix.shape[1]
        self.half = conv_full.shape[1] // 3

    def taps(self, kind):
        return pl.ds(0, 2 * self.half) if kind == OUTER else pl.ds(2 * self.half, self.half)

    def full(self, kind, source):
        if kind != MIX:
            rows = pl.ds(pl.multiple_of(source * self.depth, 16), self.depth)
            return self.conv_full.at[rows, self.taps(kind)]
        return self.mix_full.at[pl.ds(pl.multiple_of((source % 8) * self.inner, 16), self.inner), :]

    def copy(self, kind, source, mine, lane):
        spot = self.spot
        z, q, p = spot.z, spot.q, spot.p
        device = (
            spot.ctx(z, q, 1 - p), spot.ctx(z, 1 - q, p), spot.ctx(z + 1, q, p), spot.ctx(z - 1, q, p),
        )[lane]
        here = self.full(kind, source)
        if mine and kind == MIX:
            here = self.mix.at[0]
        elif mine and lane == PAIR:
            here = self.other.at[:, self.taps(kind)]
        return pltpu.make_async_remote_copy(
            src_ref=here,
            dst_ref=self.full(kind, source),
            send_sem=self.send_sem.at[kind, source, lane],
            recv_sem=self.recv_sem.at[kind, source],
            device_id={"ctx": device},
            device_id_type=MESH,
        )

    def send(self, kind, source, mine, lane, act):
        z = self.spot.z
        if lane == UP:
            pl.when(z < 3)(lambda: act(self.copy(kind, source, mine, lane)))
        elif lane == DOWN:
            pl.when(z > 0)(lambda: act(self.copy(kind, source, mine, lane)))
        else:
            act(self.copy(kind, source, mine, lane))

    def own(self):
        spot = self.spot
        copies = []
        for k in range(3):
            for n, p in enumerate((spot.p, 1 - spot.p)):
                cols = pl.ds(k * self.half, self.half)
                rows = pl.ds(pl.multiple_of(spot.me * self.depth, 16), self.depth)
                copies.append(
                    pltpu.make_async_copy(
                        self.conv.at[0, k, :, pl.ds(pl.multiple_of(p * self.half, 128), self.half)],
                        self.other.at[:, cols] if n else self.conv_full.at[rows, cols],
                        self.own_sem.at[k, n],
                    )
                )
        return copies

    def own_mix(self, act):
        spot = self.spot
        pl.when(spot.z // 2 == spot.p)(
            lambda: act(pltpu.make_async_copy(self.mix.at[0], self.full(MIX, spot.me), self.own_sem.at[3, 0]))
        )

    def begin_pair(self, act):
        spot = self.spot
        self.send(OUTER, spot.me, True, PAIR, act)

        @pl.when(spot.z // 2 == 1 - spot.p)
        def _():
            self.send(MIX, spot.me, True, PAIR, act)

        self.send(LAST, spot.me, True, PAIR, act)

    def begin(self, act):
        spot = self.spot
        me = spot.me
        for lane in (UP, DOWN):
            self.send(OUTER, me, True, lane, act)
        self.send(LAST, me, True, SIDE, act)

        @pl.when(spot.z // 2 == spot.p)
        def _():
            for lane in (UP, DOWN, SIDE):
                self.send(MIX, me, True, lane, act)

        self.send(OUTER, me, True, SIDE, act)

    def onward(self, kind, source, t, sign, act):
        if t == 0:
            self.send(kind, source, False, UP, act)
            self.send(kind, source, False, DOWN, act)
        else:

            @pl.when(sign < 0)
            def _():
                self.send(kind, source, False, UP, act)

            @pl.when(sign > 0)
            def _():
                self.send(kind, source, False, DOWN, act)

    def arrive(self, kind, source):
        self.copy(kind, source, False, PAIR).wait_recv()

    def each(self, t, body):
        if t == 0:
            body(0)
            return
        z = self.spot.z

        def side(b, c):
            sign = (1 - 2 * b) * (2 * (z // 2) - 1)

            @pl.when((z + sign * t >= 0) & (z + sign * t < 4))
            def _():
                body(sign)

            return c

        lax.fori_loop(0, 2, side, 0)

    def hop(self, t, sign, act, wait):
        spot = self.spot
        z, q, p = spot.z + sign * t, spot.q, spot.p
        for dp in (0, 1) if t else (1,):
            near = spot.ctx(z, q, 1 - p if dp else p)
            if wait:
                self.arrive(OUTER, near)
            self.onward(OUTER, near, t, sign, act)
            self.send(OUTER, near, False, SIDE, act)

            @pl.when(z // 2 == p)
            def _():
                if wait:
                    self.arrive(MIX, near)
                self.onward(MIX, near, t, sign, act)
                self.send(MIX, near, False, SIDE, act)

            if t == 0:
                if wait:
                    self.arrive(LAST, near)
                self.send(LAST, near, False, SIDE, act)

    def hop_last(self, t, sign, act, wait):
        spot = self.spot
        z = spot.z + sign * t
        for q in (spot.q, 1 - spot.q):
            for p in (spot.p, 1 - spot.p):
                source = spot.ctx(z, q, p)
                if wait:
                    self.arrive(LAST, source)
                self.onward(LAST, source, t, sign, act)

    def launch_last(self, t, act, wait):
        spot = self.spot
        for lane, ready in ((DOWN, spot.z + t == 3), (UP, spot.z == t)):

            @pl.when(ready)
            def _():
                for q in (0, 1):
                    for p in (0, 1):
                        self.send(LAST, spot.ctx(spot.z, q, p), False, lane, act)

    def side_last(self):
        spot = self.spot
        for p in (0, 1):
            self.arrive(LAST, spot.ctx(spot.z, 1 - spot.q, p))

    def rest(self, z):
        spot = self.spot
        for p in (0, 1):
            far = spot.ctx(z, 1 - spot.q, p)
            self.arrive(OUTER, far)

            @pl.when(z // 2 == spot.p)
            def _():
                self.arrive(MIX, far)

    def sent(self):
        def act(copy):
            copy.wait_send()

        self.begin_pair(act)
        self.begin(act)
        for t in range(4):
            self.each(t, lambda sign: self.hop(t, sign, act, False))
            self.launch_last(t, act, False)
            if t:
                self.each(t, lambda sign: self.hop_last(t, sign, act, False))


class Edges:
    def __init__(self, spot, level, source, first, buffer, send_sem, recv_sem):
        self.me, self.level, self.source, self.first, self.buffer = spot.me, level, source, first, buffer
        self.send_sem, self.recv_sem = send_sem, recv_sem
        self.rows = buffer.shape[1] - 2 * EDGE
        self.same = level is spot.level
        self.section = level

    def land(self, side, slot):
        return self.buffer.at[slot, pl.ds(0 if side == 0 else EDGE + self.rows, EDGE), :]

    def sends(self, remote, local):
        for side in (0, 1):
            there = self.me < 15 if side == 0 else self.me > 0
            near = self.me + 1 if side == 0 else self.me - 1
            for slot in (0, 1):
                target = near if slot == 0 else mate(near)
                start = self.first + (self.rows - EDGE if side == 0 else 0)
                source = self.source(start)
                copy = pltpu.make_async_remote_copy(
                    src_ref=source,
                    dst_ref=self.land(side, slot),
                    send_sem=self.send_sem.at[side, slot],
                    recv_sem=self.recv_sem.at[side, slot],
                    device_id={"ctx": target, "section": self.section},
                    device_id_type=MESH,
                )
                if slot == 0 or not self.same:
                    pl.when(there)(lambda: remote(copy))
                else:
                    pl.when(there & (target != self.me))(lambda: remote(copy))
                    if local is not None:
                        pl.when(there & (target == self.me))(
                            lambda: local(
                                pltpu.make_async_copy(source, self.land(side, slot), self.recv_sem.at[side, slot])
                            )
                        )

    def start(self):
        self.sends(lambda c: c.start(), lambda c: c.start())

    def sent(self):
        self.sends(lambda c: c.wait_send(), None)

    def receive(self):
        for slot in (0, 1):
            block = self.me if slot == 0 else mate(self.me)
            for side in (0, 1):
                there = block > 0 if side == 0 else block < 15
                giver = block - 1 if side == 0 else block + 1
                land = self.land(side, slot)
                source = self.buffer.at[0, pl.ds(EDGE, EDGE), :]

                arrived = pltpu.make_async_remote_copy(
                    src_ref=source,
                    dst_ref=land,
                    send_sem=self.send_sem.at[side, slot],
                    recv_sem=self.recv_sem.at[side, slot],
                    device_id={"ctx": giver, "section": 1},
                    device_id_type=MESH,
                )
                if self.same:
                    pl.when(there & (giver != self.me))(arrived.wait_recv)
                    pl.when(there & (giver == self.me))(
                        pltpu.make_async_copy(source, land, self.recv_sem.at[side, slot]).wait
                    )
                else:
                    pl.when(there)(arrived.wait_recv)

                @pl.when(jnp.logical_not(there))
                def _():
                    land[...] = jnp.zeros(land.shape, land.dtype)


def columns(count, width, body):
    def step(n, c):
        body(pl.ds(pl.multiple_of(n * width, width), width), n)
        return c

    lax.fori_loop(0, count, step, 0)


def across(left, right):
    return lax.dot_general(left, right, (((1,), (1,)), ((), ())), preferred_element_type=jnp.float32)


def tower_kernel(
    conv_w, mix_w, inputs, scale_in, shift_in, cotangent, out,
    conv_full, mix_full, other, held, scale, shift, factor, hidden, grad, conv_sum, back, dpadded, dconv, dtotal, part_out, part_in, result,
    send_sem, recv_sem, own_sem, load_sem, hid_send, hid_recv, edge_send, edge_recv, cot_send, cot_recv, cedge_send, cedge_recv,
    grad_send, grad_recv, gedge_send, gedge_recv, part_send, part_recv, out_sem, gates,
):
    spot = Spot()
    level, me = spot.level, spot.me
    rows, wide = cotangent.shape
    half = conv_full.shape[1] // 3
    plane = wide // 4
    tall = rows + 2 * EDGE
    tiles = wide // TILE
    middle = pl.ds(EDGE, rows)
    partner = spot.ctx(spot.z, spot.q, 1 - spot.p)
    gather = Gather(spot, conv_w, mix_w, conv_full, mix_full, other, send_sem, recv_sem, own_sem)

    def start(copy):
        copy.start()

    loads = [
        pltpu.make_async_copy(inputs.at[0], held, load_sem.at[0]),
        pltpu.make_async_copy(scale_in, scale, load_sem.at[2]),
        pltpu.make_async_copy(shift_in, shift, load_sem.at[3]),
    ]
    own = gather.own()
    for copy in own + loads:
        copy.start()
    gather.own_mix(start)
    load_cot = pltpu.make_async_copy(cotangent, grad.at[0, middle, :], load_sem.at[1])
    pl.when(level == 1)(load_cot.start)
    greet(spot)
    for copy in own:
        copy.wait()

    def cot_copy():
        return pltpu.make_async_remote_copy(
            src_ref=cotangent, dst_ref=grad.at[1, middle, :], send_sem=cot_send, recv_sem=cot_recv,
            device_id={"ctx": partner}, device_id_type=MESH,
        )

    cot_edges = Edges(spot, level, lambda r: cotangent.at[pl.ds(r, EDGE), :], 0, grad, cedge_send, cedge_recv)

    ends = (spot.z == 0) | (spot.z == 3)

    @pl.when(level == 1)
    def _():
        gather.begin(start)
        gather.begin_pair(start)

    for copy in loads:
        copy.wait()

    def front(cols, _):
        gain = scale[:, cols]
        pre = held[:, cols].astype(jnp.float32) * gain + shift[:, cols]
        act, slope = gelu_parts(pre)
        hidden[0, middle, cols] = act.astype(jnp.bfloat16)
        factor[:, cols] = slope * gain

    columns(wide // LANES, LANES, front)

    def hid_copy():
        return pltpu.make_async_remote_copy(
            src_ref=hidden.at[0, middle, :], dst_ref=hidden.at[1, middle, :], send_sem=hid_send, recv_sem=hid_recv,
            device_id={"ctx": partner}, device_id_type=MESH,
        )

    edges = Edges(spot, level, lambda r: hidden.at[0, pl.ds(r, EDGE), :], EDGE, hidden, edge_send, edge_recv)

    def pair_part():
        pl.semaphore_wait(gates.at[0], 1)
        gather.begin_pair(start)
        hid_copy().start()
        edges.start()

    def rest_part():
        pl.semaphore_wait(gates.at[1], 1)
        gather.begin(start)

    @pl.when(level == 1)
    def _():
        hid_copy().start()
        edges.start()
        cot_copy().start()
        cot_edges.start()

    gather.own_mix(lambda c: c.wait())

    @pl.when((level == 0) & ends)
    def _():
        rest_part()
        pair_part()

    @pl.when((level == 0) & jnp.logical_not(ends))
    def _():
        pair_part()
        rest_part()

    def add_half(here, cols):
        off = pl.ds(pl.multiple_of(2 * here * plane, 2 * plane), 2 * plane)
        near = here is mine

        def slot(n, c):
            term = jnp.dot(hidden[n, :, off], conv_full[off, cols], preferred_element_type=jnp.float32)
            if near:
                conv_sum[n, :, cols] = term
            else:
                conv_sum[n, :, cols] += term
            return c

        lax.fori_loop(0, 2, slot, 0)

    mine = spot.z // 2

    def grad_copy(n, slot):
        cols = pl.ds(n * TILE, TILE)
        return pltpu.make_async_remote_copy(
            src_ref=result.at[:, cols],
            dst_ref=grad.at[slot, middle, cols],
            send_sem=grad_send.at[n, slot],
            recv_sem=grad_recv.at[n, slot],
            device_id={"ctx": me if slot == 0 else mate(me), "section": 0},
            device_id_type=MESH,
        )

    grad_edges = Edges(spot, 0, lambda r: result.at[pl.ds(r, EDGE), :], 0, grad, gedge_send, gedge_recv)

    def pull(n, c):
        back[n] = across(grad[n], mix_full[...])
        return c

    def open_gates(stage):
        for gate, place in ((0, "pair"), (1, "ends"), (1, "inner")):
            if stage == GATES[place]:
                who = {"pair": True, "ends": ends, "inner": jnp.logical_not(ends)}[place]

                @pl.when((level == 1) & who)
                def _():
                    pl.semaphore_signal(gates.at[gate], inc=1, device_id={"section": 0}, device_id_type=MESH)

    for t in range(4):
        gather.each(t, lambda sign: gather.hop(t, sign, start, True))
        if t == 0:
            gather.side_last()
        gather.launch_last(t, start, True)
        open_gates(t)

    for t in (1, 2):
        gather.each(t, lambda sign: gather.hop_last(t, sign, start, True))
        open_gates(3 + t)

    hid_copy().wait_recv()
    edges.receive()
    for k in range(2):
        gather.rest(2 * mine + k)
    add_half(mine, pl.ds(0, 3 * half))
    open_gates(6)
    for k in range(2):
        gather.rest(2 * (1 - mine) + k)
    add_half(1 - mine, gather.taps(OUTER))

    @pl.when(level == 1)
    def _():
        load_cot.wait()
        cot_copy().wait_recv()
        cot_edges.receive()

    @pl.when(level == 0)
    def _():
        for n in range(tiles):
            for slot in (0, 1):
                grad_copy(n, slot).wait_recv()
        grad_edges.receive()

    lax.fori_loop(0, 2, pull, 0)
    gather.each(3, lambda sign: gather.hop_last(3, sign, start, True))
    add_half(1 - mine, gather.taps(LAST))

    low, count = EDGE // 2, rows + EDGE

    def slopes(m):
        cols, c0, c1, c2 = (pl.ds(m * LANES + k * half, LANES) for k in (0, 0, 1, 2))
        for n in range(2):
            near = conv_sum[n, low - 1:low - 1 + count, c0] + conv_sum[n, low + 1:low + 1 + count, c2]
            far = conv_sum[n, low - 2:low - 2 + count, c0] + conv_sum[n, low + 2:low + 2 + count, c2]
            conv = jnp.where(level == 0, near, far) + conv_sum[n, low:low + count, c1]
            value = back[n, low:low + count, cols] * gelu_parts(conv)[1]
            dpadded[n, low:low + count, cols] = value.astype(jnp.bfloat16).astype(jnp.float32)
            there = pl.ds(n * rows, rows)
            dconv[there, c1] = dpadded[n, EDGE:EDGE + rows, cols].astype(jnp.bfloat16)
            near = dpadded[n, EDGE + 1:EDGE + 1 + rows, cols]
            far = dpadded[n, EDGE + 2:EDGE + 2 + rows, cols]
            dconv[there, c0] = jnp.where(level == 0, near, far).astype(jnp.bfloat16)
            near = dpadded[n, EDGE - 1:EDGE - 1 + rows, cols]
            far = dpadded[n, EDGE - 2:EDGE - 2 + rows, cols]
            dconv[there, c2] = jnp.where(level == 0, near, far).astype(jnp.bfloat16)

    for m in range(half // LANES):
        slopes(m)

    def part_copy(n):
        return pltpu.make_async_remote_copy(
            src_ref=part_out.at[n], dst_ref=part_in.at[n], send_sem=part_send.at[n], recv_sem=part_recv.at[n],
            device_id={"ctx": partner}, device_id_type=MESH,
        )

    def out_copy(n):
        cols = pl.ds(n * TILE, TILE)
        return pltpu.make_async_copy(result.at[:, cols], out.at[0, :, cols], out_sem.at[n])

    def settle():
        hid_copy().wait_send()
        edges.sent()
        gather.sent()

        @pl.when(level == 1)
        def _():
            cot_copy().wait_send()
            cot_edges.sent()

    for n in range(tiles + BEHIND):
        if n < tiles:
            cols = pl.ds(n * TILE, TILE)
            term = across(dconv[...], conv_full[cols, :])
            part_out[n] = term[rows:].astype(jnp.bfloat16)
            dtotal[:, cols] = term[:rows]
            part_copy(n).start()
        if n == tiles - 1:
            settle()
        m = n - BEHIND
        if m >= 0:
            cols = pl.ds(m * TILE, TILE)
            part_copy(m).wait_recv()
            dhidden = dtotal[:, cols] + part_in[m].astype(jnp.float32)
            result[:, cols] = (
                grad[0, middle, cols].astype(jnp.float32) + dhidden * factor[:, cols]
            ).astype(jnp.bfloat16)
            out_copy(m).start()

            @pl.when(level == 1)
            def _():
                grad_copy(m, 0).start()
                grad_copy(m, 1).start()

    @pl.when(level == 1)
    def _():
        grad_edges.start()
    for n in range(tiles):
        part_copy(n).wait_send()
        out_copy(n).wait()

    @pl.when(level == 1)
    def _():
        for n in range(tiles):
            for slot in (0, 1):
                grad_copy(n, slot).wait_send()
        grad_edges.sent()


def tower(layer_inputs, conv_weight, mix_weight, bn_scale, bn_shift, cotangent):
    rows, wide = cotangent.shape
    inner = conv_weight.shape[3]
    half = inner // 2
    tall = rows + 2 * EDGE
    tiles = wide // TILE
    anywhere = pl.BlockSpec(memory_space=pl.ANY)
    bf16, f32 = jnp.bfloat16, jnp.float32
    dma = pltpu.SemaphoreType.DMA
    return pl.pallas_call(
        tower_kernel,
        out_shape=jax.ShapeDtypeStruct(layer_inputs.shape, bf16),
        in_specs=[anywhere] * 6,
        out_specs=anywhere,
        scratch_shapes=[
            pltpu.VMEM((wide, 3 * half), bf16),
            pltpu.VMEM((half, wide), bf16),
            pltpu.VMEM((conv_weight.shape[2], 3 * half), bf16),
            pltpu.VMEM((rows, wide), bf16),
            pltpu.VMEM((1, wide), f32),
            pltpu.VMEM((1, wide), f32),
            pltpu.VMEM((rows, wide), f32),
            pltpu.VMEM((2, tall, wide), bf16),
            pltpu.VMEM((2, tall, wide), bf16),
            pltpu.VMEM((2, tall, 3 * half), f32),
            pltpu.VMEM((2, tall, half), f32),
            pltpu.VMEM((2, tall, half), f32),
            pltpu.VMEM((2 * rows, 3 * half), bf16),
            pltpu.VMEM((rows, wide), f32),
            pltpu.VMEM((tiles, rows, TILE), bf16),
            pltpu.VMEM((tiles, rows, TILE), bf16),
            pltpu.VMEM((rows, wide), bf16),
            dma((3, 16, 4)),
            dma((3, 16)),
            dma((4, 2)),
            dma((4,)),
            dma,
            dma,
            dma((2, 2)),
            dma((2, 2)),
            dma,
            dma,
            dma((2, 2)),
            dma((2, 2)),
            dma((tiles, 2)),
            dma((tiles, 2)),
            dma((2, 2)),
            dma((2, 2)),
            dma((tiles,)),
            dma((tiles,)),
            dma((tiles,)),
            pltpu.SemaphoreType.REGULAR((2,)),
        ],
        compiler_params=pltpu.CompilerParams(
            collective_id=0, has_side_effects=True, vmem_limit_bytes=64 * 1024 * 1024
        ),
    )(conv_weight, mix_weight, layer_inputs, bn_scale, bn_shift, cotangent)


def extended(cells, sides, width):
    for axis, dim in sides:
        count = lax.axis_size(axis)
        ends = count - 1
        head = lax.slice_in_dim(cells, 0, width, axis=dim)
        tail = lax.slice_in_dim(cells, cells.shape[dim] - width, cells.shape[dim], axis=dim)
        cells = jnp.concatenate(
            [
                lax.ppermute(tail, axis, [(i, (i + 1) % count) for i in range(ends)]),
                cells,
                lax.ppermute(head, axis, [((i + 1) % count, i) for i in range(ends)]),
            ],
            axis=dim,
        )
    return cells


def shifted(block, axis, distance):
    devices = range(lax.axis_size(axis))
    route = [(i - distance, i) for i in devices if i - distance in devices]
    return lax.ppermute(block, axis, route)


def gelu_parts(value):
    cdf = 0.5 * (1.0 + lax.erf(value * 0.7071067811865476))
    dens = jnp.exp(-0.5 * value * value) * 0.3989422804014327
    return (value * cdf, cdf + value * dens)


def shards(layer_inputs, conv_weight, mix_weight, bn_scale, bn_shift, cotangent):
    sections = lax.axis_size("section")
    level = lax.axis_index("section")
    widest = 2 ** (sections - 1)
    if lax.axis_size("ctx") == 16 and sections == 2:
        return tower(layer_inputs, conv_weight, mix_weight, bn_scale, bn_shift, cotangent)
    conv_full = lax.all_gather(conv_weight, "ctx", axis=2, tiled=True)[0]
    mix_full = lax.all_gather(mix_weight, "ctx", axis=1, tiled=True)[0]
    rows = cotangent.shape[0]
    inner = mix_full.shape[0]
    spacing = jnp.left_shift(jnp.int32(1), level)
    pre = layer_inputs[0].astype(jnp.float32) * bn_scale[0] + bn_shift[0]
    act, slope_pre = gelu_parts(pre)
    hidden = act.astype(jnp.bfloat16)
    padded = extended(hidden, (("ctx", 0),), widest)
    conv = jnp.zeros((rows, inner), jnp.float32)
    for k in range(3):
        window = lax.dynamic_slice_in_dim(padded, widest + (k - 1) * spacing, rows, 0)
        conv = conv + jnp.dot(window, conv_full[k], preferred_element_type=jnp.float32)
    _, slope_conv = gelu_parts(conv)
    factor = slope_pre * bn_scale[0]

    def make_dconv(grad):
        back = jnp.einsum("pc,hc->ph", grad, mix_full, preferred_element_type=jnp.float32)
        return (back * slope_conv).astype(jnp.bfloat16)

    def skip_dconv(grad):
        return jnp.zeros((rows, inner), jnp.bfloat16)

    def finish(grad, dpad, starts):
        dhidden = jnp.zeros((rows, conv_full.shape[1]), jnp.float32)
        for k in range(3):
            window = lax.dynamic_slice_in_dim(dpad, starts[k], rows, 0)
            dhidden = dhidden + jnp.einsum(
                "ph,ch->pc", window, conv_full[k], preferred_element_type=jnp.float32
            )
        return (grad.astype(jnp.float32) + dhidden * factor).astype(jnp.bfloat16)

    mine = jnp.zeros_like(cotangent)

    def turn(step, carry):
        grad, mine = carry
        active = level == sections - 1 - step
        dconv = lax.cond(active, make_dconv, skip_dconv, grad)
        dpad = extended(dconv, (("ctx", 0),), widest)
        starts = [widest + (1 - k) * spacing for k in range(3)]
        result = lax.cond(active, lambda g: finish(g, dpad, starts), lambda g: g, grad)
        mine = jnp.where(active, result, mine)
        grad = shifted(result, "section", -1)
        return (grad, mine)

    grad, mine = lax.fori_loop(0, sections, turn, (cotangent, mine))
    return mine[None]


def solution(mesh):
    return jax.shard_map(
        shards,
        mesh=mesh,
        in_specs=(
            P("section", "ctx", None),
            P("section", None, "ctx", None),
            P("section", "ctx", None),
            P("section", None),
            P("section", None),
            P("ctx", None),
        ),
        out_specs=P("section", "ctx", None),
        check_vma=False,
    )
```

```python
import jax
import jax.numpy as jnp
from jax import lax
from jax.experimental import pallas as pl
from jax.experimental.pallas import tpu as pltpu
from jax.sharding import PartitionSpec as P

MESH = pl.DeviceIdType.MESH
EDGE = 16
LANES = 128
TILE = 256
DEVICES = 32
GATES = {"pair": 3, "ends": 1, "inner": 5}
BEHIND = 4


def mate(c):
    return c + 1 - 2 * (c % 2)


class Spot:
    def __init__(self):
        self.level = lax.axis_index("section")
        self.me = me = lax.axis_index("ctx")
        self.z, self.q, self.p = me // 4, (me // 2) % 2, me % 2

    def ctx(self, z, q, p):
        return z * 4 + q * 2 + p


def greet(spot):
    barrier = pltpu.get_barrier_semaphore()
    index = spot.me * 2 + spot.level

    def hello(k, c):
        device = (index + k) % DEVICES
        pl.semaphore_signal(
            barrier, inc=1, device_id={"ctx": device // 2, "section": device % 2}, device_id_type=MESH
        )
        return c

    lax.fori_loop(1, DEVICES, hello, 0)
    pl.semaphore_wait(barrier, DEVICES - 1)


PAIR, SIDE, UP, DOWN = range(4)
OUTER, LAST, MIX, PLANE = range(4)


class Gather:
    def __init__(self, spot, conv, mix, conv_full, mix_full, other, send_sem, recv_sem, own_sem):
        self.spot, self.conv, self.mix, self.conv_full, self.mix_full = spot, conv, mix, conv_full, mix_full
        self.other, self.send_sem, self.recv_sem, self.own_sem = other, send_sem, recv_sem, own_sem
        self.depth, self.inner = conv.shape[2], mix.shape[1]
        self.half = conv_full.shape[1] // 3

    def taps(self, kind):
        return pl.ds(0, 2 * self.half) if kind == OUTER else pl.ds(2 * self.half, self.half)

    def full(self, kind, source):
        if kind == PLANE:
            return self.conv_full.at[pl.ds(pl.multiple_of(source * self.depth, 16), 4 * self.depth), self.taps(LAST)]
        if kind != MIX:
            rows = pl.ds(pl.multiple_of(source * self.depth, 16), self.depth)
            return self.conv_full.at[rows, self.taps(kind)]
        return self.mix_full.at[pl.ds(pl.multiple_of((source % 8) * self.inner, 16), self.inner), :]

    def leaving(self, kind, source, lane):
        z, p = source // 4, source % 2
        if kind == PLANE:
            return 41 + z + (lane == DOWN)
        if kind == LAST:
            return 38 if lane == PAIR else 39 + p
        first = 0 if kind == OUTER else 19
        if lane == PAIR:
            return first + 18
        if lane == SIDE:
            return first + 10 + 2 * z + p
        return first + 2 * (z + (lane == DOWN)) + p

    def coming(self, kind, source):
        if kind == OUTER:
            return source
        if kind == MIX:
            return 16 + source % 8
        return 24 + source % 4 if kind == LAST else 28 + source // 4

    def copy(self, kind, source, mine, lane):
        spot = self.spot
        z, q, p = spot.z, spot.q, spot.p
        device = (
            spot.ctx(z, q, 1 - p), spot.ctx(z, 1 - q, p), spot.ctx(z + 1, q, p), spot.ctx(z - 1, q, p),
        )[lane]
        here = self.full(kind, source)
        if mine and kind == MIX:
            here = self.mix.at[0]
        elif mine and lane == PAIR:
            here = self.other.at[:, self.taps(kind)]
        return pltpu.make_async_remote_copy(
            src_ref=here,
            dst_ref=self.full(kind, source),
            send_sem=self.send_sem.at[self.leaving(kind, source, lane)],
            recv_sem=self.recv_sem.at[self.coming(kind, source)],
            device_id={"ctx": device},
            device_id_type=MESH,
        )

    def send(self, kind, source, mine, lane, act):
        z = self.spot.z
        if lane == UP:
            pl.when(z < 3)(lambda: act(self.copy(kind, source, mine, lane)))
        elif lane == DOWN:
            pl.when(z > 0)(lambda: act(self.copy(kind, source, mine, lane)))
        else:
            act(self.copy(kind, source, mine, lane))

    def own(self):
        spot = self.spot
        copies = []
        for k in range(3):
            for n, p in enumerate((spot.p, 1 - spot.p)):
                cols = pl.ds(k * self.half, self.half)
                rows = pl.ds(pl.multiple_of(spot.me * self.depth, 16), self.depth)
                copies.append(
                    pltpu.make_async_copy(
                        self.conv.at[0, k, :, pl.ds(pl.multiple_of(p * self.half, 128), self.half)],
                        self.other.at[:, cols] if n else self.conv_full.at[rows, cols],
                        self.own_sem.at[k, n],
                    )
                )
        return copies

    def own_mix(self, act):
        spot = self.spot
        pl.when(spot.z // 2 == spot.p)(
            lambda: act(pltpu.make_async_copy(self.mix.at[0], self.full(MIX, spot.me), self.own_sem.at[3, 0]))
        )

    def begin_pair(self, act):
        spot = self.spot
        self.send(OUTER, spot.me, True, PAIR, act)

        @pl.when(spot.z // 2 == 1 - spot.p)
        def _():
            self.send(MIX, spot.me, True, PAIR, act)

        self.send(LAST, spot.me, True, PAIR, act)

    def begin(self, act):
        spot = self.spot
        me = spot.me
        for lane in (UP, DOWN):
            self.send(OUTER, me, True, lane, act)
        self.send(LAST, me, True, SIDE, act)

        @pl.when(spot.z // 2 == spot.p)
        def _():
            for lane in (UP, DOWN, SIDE):
                self.send(MIX, me, True, lane, act)

        self.send(OUTER, me, True, SIDE, act)

    def onward(self, kind, source, t, sign, act):
        if t == 0:
            self.send(kind, source, False, UP, act)
            self.send(kind, source, False, DOWN, act)
        else:

            @pl.when(sign < 0)
            def _():
                self.send(kind, source, False, UP, act)

            @pl.when(sign > 0)
            def _():
                self.send(kind, source, False, DOWN, act)

    def arrive(self, kind, source):
        self.copy(kind, source, False, PAIR).wait_recv()

    def each(self, t, body):
        if t == 0:
            body(0)
            return
        z = self.spot.z

        def side(b, c):
            sign = (1 - 2 * b) * (2 * (z // 2) - 1)

            @pl.when((z + sign * t >= 0) & (z + sign * t < 4))
            def _():
                body(sign)

            return c

        lax.fori_loop(0, 2, side, 0)

    def hop(self, t, sign, act, wait):
        spot = self.spot
        z, q, p = spot.z + sign * t, spot.q, spot.p
        for dp in (0, 1) if t else (1,):
            near = spot.ctx(z, q, 1 - p if dp else p)
            if wait:
                self.arrive(OUTER, near)
            self.onward(OUTER, near, t, sign, act)
            self.send(OUTER, near, False, SIDE, act)

            @pl.when(z // 2 == p)
            def _():
                if wait:
                    self.arrive(MIX, near)
                self.onward(MIX, near, t, sign, act)
                self.send(MIX, near, False, SIDE, act)

            if t == 0:
                if wait:
                    self.arrive(LAST, near)
                self.send(LAST, near, False, SIDE, act)

    def hop_last(self, t, sign, act, wait):
        spot = self.spot
        z = spot.z + sign * t
        if wait:
            self.arrive(PLANE, z * 4)
        self.onward(PLANE, z * 4, t, sign, act)

    def launch_last(self, t, act, wait):
        spot = self.spot
        for lane, ready in ((DOWN, spot.z + t == 3), (UP, spot.z == t)):

            @pl.when(ready)
            def _():
                self.send(PLANE, spot.z * 4, False, lane, act)

    def side_last(self):
        spot = self.spot
        for p in (0, 1):
            self.arrive(LAST, spot.ctx(spot.z, 1 - spot.q, p))

    def rest(self, z):
        spot = self.spot
        for p in (0, 1):
            far = spot.ctx(z, 1 - spot.q, p)
            self.arrive(OUTER, far)

            @pl.when(z // 2 == spot.p)
            def _():
                self.arrive(MIX, far)

    def sent(self):
        def act(copy):
            copy.wait_send()

        self.begin_pair(act)
        self.begin(act)
        for t in range(4):
            self.each(t, lambda sign: self.hop(t, sign, act, False))
            self.launch_last(t, act, False)
            if t:
                self.each(t, lambda sign: self.hop_last(t, sign, act, False))


class Edges:
    def __init__(self, spot, level, source, first, buffer, send_sem, recv_sem):
        self.me, self.level, self.source, self.first, self.buffer = spot.me, level, source, first, buffer
        self.send_sem, self.recv_sem = send_sem, recv_sem
        self.rows = buffer.shape[1] - 2 * EDGE
        self.same = level is spot.level
        self.section = level

    def land(self, side, slot):
        return self.buffer.at[slot, pl.ds(0 if side == 0 else EDGE + self.rows, EDGE), :]

    def sends(self, remote, local):
        for side in (0, 1):
            there = self.me < 15 if side == 0 else self.me > 0
            near = self.me + 1 if side == 0 else self.me - 1
            for slot in (0, 1):
                target = near if slot == 0 else mate(near)
                start = self.first + (self.rows - EDGE if side == 0 else 0)
                source = self.source(start)
                copy = pltpu.make_async_remote_copy(
                    src_ref=source,
                    dst_ref=self.land(side, slot),
                    send_sem=self.send_sem.at[side, slot],
                    recv_sem=self.recv_sem.at[side, slot],
                    device_id={"ctx": target, "section": self.section},
                    device_id_type=MESH,
                )
                if slot == 0 or not self.same:
                    pl.when(there)(lambda: remote(copy))
                else:
                    pl.when(there & (target != self.me))(lambda: remote(copy))
                    if local is not None:
                        pl.when(there & (target == self.me))(
                            lambda: local(
                                pltpu.make_async_copy(source, self.land(side, slot), self.recv_sem.at[side, slot])
                            )
                        )

    def start(self):
        self.sends(lambda c: c.start(), lambda c: c.start())

    def sent(self):
        self.sends(lambda c: c.wait_send(), None)

    def receive(self):
        for slot in (0, 1):
            block = self.me if slot == 0 else mate(self.me)
            for side in (0, 1):
                there = block > 0 if side == 0 else block < 15
                giver = block - 1 if side == 0 else block + 1
                land = self.land(side, slot)
                source = self.buffer.at[0, pl.ds(EDGE, EDGE), :]

                arrived = pltpu.make_async_remote_copy(
                    src_ref=source,
                    dst_ref=land,
                    send_sem=self.send_sem.at[side, slot],
                    recv_sem=self.recv_sem.at[side, slot],
                    device_id={"ctx": giver, "section": 1},
                    device_id_type=MESH,
                )
                if self.same:
                    pl.when(there & (giver != self.me))(arrived.wait_recv)
                    pl.when(there & (giver == self.me))(
                        pltpu.make_async_copy(source, land, self.recv_sem.at[side, slot]).wait
                    )
                else:
                    pl.when(there)(arrived.wait_recv)

                @pl.when(jnp.logical_not(there))
                def _():
                    land[...] = jnp.zeros(land.shape, land.dtype)


def columns(count, width, body):
    def step(n, c):
        body(pl.ds(pl.multiple_of(n * width, width), width), n)
        return c

    lax.fori_loop(0, count, step, 0)


def across(left, right):
    return lax.dot_general(left, right, (((1,), (1,)), ((), ())), preferred_element_type=jnp.float32)


def tower_kernel(
    conv_w, mix_w, inputs, scale_in, shift_in, cotangent, out,
    conv_full, mix_full, other, held, scale, shift, factor, hidden, grad, conv_sum, back, dpadded, dconv, dtotal, part_out, part_in, result,
    send_sem, recv_sem, own_sem, load_sem, hid_send, hid_recv, edge_send, edge_recv, cot_send, cot_recv, cedge_send, cedge_recv,
    grad_send, grad_recv, gedge_send, gedge_recv, part_send, part_recv, out_sem, gates,
):
    spot = Spot()
    level, me = spot.level, spot.me
    rows, wide = cotangent.shape
    half = conv_full.shape[1] // 3
    plane = wide // 4
    tall = rows + 2 * EDGE
    tiles = wide // TILE
    middle = pl.ds(EDGE, rows)
    partner = spot.ctx(spot.z, spot.q, 1 - spot.p)
    gather = Gather(spot, conv_w, mix_w, conv_full, mix_full, other, send_sem, recv_sem, own_sem)

    def start(copy):
        copy.start()

    loads = [
        pltpu.make_async_copy(inputs.at[0], held, load_sem.at[0]),
        pltpu.make_async_copy(scale_in, scale, load_sem.at[2]),
        pltpu.make_async_copy(shift_in, shift, load_sem.at[3]),
    ]
    own = gather.own()
    for copy in own + loads:
        copy.start()
    gather.own_mix(start)
    load_cot = pltpu.make_async_copy(cotangent, grad.at[0, middle, :], load_sem.at[1])
    pl.when(level == 1)(load_cot.start)
    greet(spot)
    for copy in own:
        copy.wait()

    def cot_copy():
        return pltpu.make_async_remote_copy(
            src_ref=cotangent, dst_ref=grad.at[1, middle, :], send_sem=cot_send, recv_sem=cot_recv,
            device_id={"ctx": partner}, device_id_type=MESH,
        )

    cot_edges = Edges(spot, level, lambda r: cotangent.at[pl.ds(r, EDGE), :], 0, grad, cedge_send, cedge_recv)

    ends = (spot.z == 0) | (spot.z == 3)

    @pl.when(level == 1)
    def _():
        gather.begin(start)
        gather.begin_pair(start)

    for copy in loads:
        copy.wait()

    def front(cols, _):
        gain = scale[:, cols]
        pre = held[:, cols].astype(jnp.float32) * gain + shift[:, cols]
        act, slope = gelu_parts(pre)
        hidden[0, middle, cols] = act.astype(jnp.bfloat16)
        factor[:, cols] = slope * gain

    columns(wide // LANES, LANES, front)

    def hid_copy():
        return pltpu.make_async_remote_copy(
            src_ref=hidden.at[0, middle, :], dst_ref=hidden.at[1, middle, :], send_sem=hid_send, recv_sem=hid_recv,
            device_id={"ctx": partner}, device_id_type=MESH,
        )

    edges = Edges(spot, level, lambda r: hidden.at[0, pl.ds(r, EDGE), :], EDGE, hidden, edge_send, edge_recv)

    def pair_part():
        pl.semaphore_wait(gates.at[0], 1)
        gather.begin_pair(start)
        hid_copy().start()
        edges.start()

    def rest_part():
        pl.semaphore_wait(gates.at[1], 1)
        gather.begin(start)

    @pl.when(level == 1)
    def _():
        hid_copy().start()
        edges.start()
        cot_copy().start()
        cot_edges.start()

    gather.own_mix(lambda c: c.wait())

    @pl.when((level == 0) & ends)
    def _():
        rest_part()
        pair_part()

    @pl.when((level == 0) & jnp.logical_not(ends))
    def _():
        pair_part()
        rest_part()

    def add_half(here, cols):
        off = pl.ds(pl.multiple_of(2 * here * plane, 2 * plane), 2 * plane)
        near = here is mine

        def slot(n, c):
            term = jnp.dot(hidden[n, :, off], conv_full[off, cols], preferred_element_type=jnp.float32)
            if near:
                conv_sum[n, :, cols] = term
            else:
                conv_sum[n, :, cols] += term
            return c

        lax.fori_loop(0, 2, slot, 0)

    mine = spot.z // 2

    def grad_copy(n, slot):
        cols = pl.ds(n * TILE, TILE)
        return pltpu.make_async_remote_copy(
            src_ref=result.at[:, cols],
            dst_ref=grad.at[slot, middle, cols],
            send_sem=grad_send.at[n, slot],
            recv_sem=grad_recv.at[n, slot],
            device_id={"ctx": me if slot == 0 else mate(me), "section": 0},
            device_id_type=MESH,
        )

    grad_edges = Edges(spot, 0, lambda r: result.at[pl.ds(r, EDGE), :], 0, grad, gedge_send, gedge_recv)

    def pull(n, c):
        back[n] = across(grad[n], mix_full[...])
        return c

    def open_gates(stage):
        for gate, place in ((0, "pair"), (1, "ends"), (1, "inner")):
            if stage == GATES[place]:
                who = {"pair": True, "ends": ends, "inner": jnp.logical_not(ends)}[place]

                @pl.when((level == 1) & who)
                def _():
                    pl.semaphore_signal(gates.at[gate], inc=1, device_id={"section": 0}, device_id_type=MESH)

    for t in range(4):
        gather.each(t, lambda sign: gather.hop(t, sign, start, True))
        if t == 0:
            gather.side_last()
        gather.launch_last(t, start, True)
        open_gates(t)

    for t in (1, 2):
        gather.each(t, lambda sign: gather.hop_last(t, sign, start, True))
        open_gates(3 + t)

    hid_copy().wait_recv()
    edges.receive()
    for k in range(2):
        gather.rest(2 * mine + k)
    add_half(mine, pl.ds(0, 3 * half))
    open_gates(6)
    for k in range(2):
        gather.rest(2 * (1 - mine) + k)
    add_half(1 - mine, gather.taps(OUTER))

    @pl.when(level == 1)
    def _():
        load_cot.wait()
        cot_copy().wait_recv()
        cot_edges.receive()

    @pl.when(level == 0)
    def _():
        for n in range(tiles):
            for slot in (0, 1):
                grad_copy(n, slot).wait_recv()
        grad_edges.receive()

    lax.fori_loop(0, 2, pull, 0)
    gather.each(3, lambda sign: gather.hop_last(3, sign, start, True))
    add_half(1 - mine, gather.taps(LAST))

    low, count = EDGE // 2, rows + EDGE

    def slopes(m):
        cols, c0, c1, c2 = (pl.ds(m * LANES + k * half, LANES) for k in (0, 0, 1, 2))
        for n in range(2):
            near = conv_sum[n, low - 1:low - 1 + count, c0] + conv_sum[n, low + 1:low + 1 + count, c2]
            far = conv_sum[n, low - 2:low - 2 + count, c0] + conv_sum[n, low + 2:low + 2 + count, c2]
            conv = jnp.where(level == 0, near, far) + conv_sum[n, low:low + count, c1]
            value = back[n, low:low + count, cols] * gelu_parts(conv)[1]
            dpadded[n, low:low + count, cols] = value.astype(jnp.bfloat16).astype(jnp.float32)
            there = pl.ds(n * rows, rows)
            dconv[there, c1] = dpadded[n, EDGE:EDGE + rows, cols].astype(jnp.bfloat16)
            near = dpadded[n, EDGE + 1:EDGE + 1 + rows, cols]
            far = dpadded[n, EDGE + 2:EDGE + 2 + rows, cols]
            dconv[there, c0] = jnp.where(level == 0, near, far).astype(jnp.bfloat16)
            near = dpadded[n, EDGE - 1:EDGE - 1 + rows, cols]
            far = dpadded[n, EDGE - 2:EDGE - 2 + rows, cols]
            dconv[there, c2] = jnp.where(level == 0, near, far).astype(jnp.bfloat16)

    for m in range(half // LANES):
        slopes(m)

    def part_copy(n):
        return pltpu.make_async_remote_copy(
            src_ref=part_out.at[n], dst_ref=part_in.at[n], send_sem=part_send.at[n], recv_sem=part_recv.at[n],
            device_id={"ctx": partner}, device_id_type=MESH,
        )

    def out_copy(n):
        cols = pl.ds(n * TILE, TILE)
        return pltpu.make_async_copy(result.at[:, cols], out.at[0, :, cols], out_sem.at[n])

    def settle():
        hid_copy().wait_send()
        edges.sent()
        gather.sent()

        @pl.when(level == 1)
        def _():
            cot_copy().wait_send()
            cot_edges.sent()

    for n in range(tiles + BEHIND):
        if n < tiles:
            cols = pl.ds(n * TILE, TILE)
            term = across(dconv[...], conv_full[cols, :])
            part_out[n] = term[rows:].astype(jnp.bfloat16)
            dtotal[:, cols] = term[:rows]
            part_copy(n).start()
        if n == tiles - 1:
            settle()
        m = n - BEHIND
        if m >= 0:
            cols = pl.ds(m * TILE, TILE)
            part_copy(m).wait_recv()
            dhidden = dtotal[:, cols] + part_in[m].astype(jnp.float32)
            result[:, cols] = (
                grad[0, middle, cols].astype(jnp.float32) + dhidden * factor[:, cols]
            ).astype(jnp.bfloat16)
            out_copy(m).start()

            @pl.when(level == 1)
            def _():
                grad_copy(m, 0).start()
                grad_copy(m, 1).start()

    @pl.when(level == 1)
    def _():
        grad_edges.start()
    for n in range(tiles):
        part_copy(n).wait_send()
        out_copy(n).wait()

    @pl.when(level == 1)
    def _():
        for n in range(tiles):
            for slot in (0, 1):
                grad_copy(n, slot).wait_send()
        grad_edges.sent()


def tower(layer_inputs, conv_weight, mix_weight, bn_scale, bn_shift, cotangent):
    rows, wide = cotangent.shape
    inner = conv_weight.shape[3]
    half = inner // 2
    tall = rows + 2 * EDGE
    tiles = wide // TILE
    anywhere = pl.BlockSpec(memory_space=pl.ANY)
    bf16, f32 = jnp.bfloat16, jnp.float32
    dma = pltpu.SemaphoreType.DMA
    return pl.pallas_call(
        tower_kernel,
        out_shape=jax.ShapeDtypeStruct(layer_inputs.shape, bf16),
        in_specs=[anywhere] * 6,
        out_specs=anywhere,
        scratch_shapes=[
            pltpu.VMEM((wide, 3 * half), bf16),
            pltpu.VMEM((half, wide), bf16),
            pltpu.VMEM((conv_weight.shape[2], 3 * half), bf16),
            pltpu.VMEM((rows, wide), bf16),
            pltpu.VMEM((1, wide), f32),
            pltpu.VMEM((1, wide), f32),
            pltpu.VMEM((rows, wide), f32),
            pltpu.VMEM((2, tall, wide), bf16),
            pltpu.VMEM((2, tall, wide), bf16),
            pltpu.VMEM((2, tall, 3 * half), f32),
            pltpu.VMEM((2, tall, half), f32),
            pltpu.VMEM((2, tall, half), f32),
            pltpu.VMEM((2 * rows, 3 * half), bf16),
            pltpu.VMEM((rows, wide), f32),
            pltpu.VMEM((tiles, rows, TILE), bf16),
            pltpu.VMEM((tiles, rows, TILE), bf16),
            pltpu.VMEM((rows, wide), bf16),
            dma((46,)),
            dma((32,)),
            dma((4, 2)),
            dma((4,)),
            dma,
            dma,
            dma((2, 2)),
            dma((2, 2)),
            dma,
            dma,
            dma((2, 2)),
            dma((2, 2)),
            dma((tiles, 2)),
            dma((tiles, 2)),
            dma((2, 2)),
            dma((2, 2)),
            dma((tiles,)),
            dma((tiles,)),
            dma((tiles,)),
            pltpu.SemaphoreType.REGULAR((2,)),
        ],
        compiler_params=pltpu.CompilerParams(
            collective_id=0, has_side_effects=True, vmem_limit_bytes=64 * 1024 * 1024
        ),
    )(conv_weight, mix_weight, layer_inputs, bn_scale, bn_shift, cotangent)


def extended(cells, sides, width):
    for axis, dim in sides:
        count = lax.axis_size(axis)
        ends = count - 1
        head = lax.slice_in_dim(cells, 0, width, axis=dim)
        tail = lax.slice_in_dim(cells, cells.shape[dim] - width, cells.shape[dim], axis=dim)
        cells = jnp.concatenate(
            [
                lax.ppermute(tail, axis, [(i, (i + 1) % count) for i in range(ends)]),
                cells,
                lax.ppermute(head, axis, [((i + 1) % count, i) for i in range(ends)]),
            ],
            axis=dim,
        )
    return cells


def shifted(block, axis, distance):
    devices = range(lax.axis_size(axis))
    route = [(i - distance, i) for i in devices if i - distance in devices]
    return lax.ppermute(block, axis, route)


def gelu_parts(value):
    cdf = 0.5 * (1.0 + lax.erf(value * 0.7071067811865476))
    dens = jnp.exp(-0.5 * value * value) * 0.3989422804014327
    return (value * cdf, cdf + value * dens)


def shards(layer_inputs, conv_weight, mix_weight, bn_scale, bn_shift, cotangent):
    sections = lax.axis_size("section")
    level = lax.axis_index("section")
    widest = 2 ** (sections - 1)
    if lax.axis_size("ctx") == 16 and sections == 2:
        return tower(layer_inputs, conv_weight, mix_weight, bn_scale, bn_shift, cotangent)
    conv_full = lax.all_gather(conv_weight, "ctx", axis=2, tiled=True)[0]
    mix_full = lax.all_gather(mix_weight, "ctx", axis=1, tiled=True)[0]
    rows = cotangent.shape[0]
    inner = mix_full.shape[0]
    spacing = jnp.left_shift(jnp.int32(1), level)
    pre = layer_inputs[0].astype(jnp.float32) * bn_scale[0] + bn_shift[0]
    act, slope_pre = gelu_parts(pre)
    hidden = act.astype(jnp.bfloat16)
    padded = extended(hidden, (("ctx", 0),), widest)
    conv = jnp.zeros((rows, inner), jnp.float32)
    for k in range(3):
        window = lax.dynamic_slice_in_dim(padded, widest + (k - 1) * spacing, rows, 0)
        conv = conv + jnp.dot(window, conv_full[k], preferred_element_type=jnp.float32)
    _, slope_conv = gelu_parts(conv)
    factor = slope_pre * bn_scale[0]

    def make_dconv(grad):
        back = jnp.einsum("pc,hc->ph", grad, mix_full, preferred_element_type=jnp.float32)
        return (back * slope_conv).astype(jnp.bfloat16)

    def skip_dconv(grad):
        return jnp.zeros((rows, inner), jnp.bfloat16)

    def finish(grad, dpad, starts):
        dhidden = jnp.zeros((rows, conv_full.shape[1]), jnp.float32)
        for k in range(3):
            window = lax.dynamic_slice_in_dim(dpad, starts[k], rows, 0)
            dhidden = dhidden + jnp.einsum(
                "ph,ch->pc", window, conv_full[k], preferred_element_type=jnp.float32
            )
        return (grad.astype(jnp.float32) + dhidden * factor).astype(jnp.bfloat16)

    mine = jnp.zeros_like(cotangent)

    def turn(step, carry):
        grad, mine = carry
        active = level == sections - 1 - step
        dconv = lax.cond(active, make_dconv, skip_dconv, grad)
        dpad = extended(dconv, (("ctx", 0),), widest)
        starts = [widest + (1 - k) * spacing for k in range(3)]
        result = lax.cond(active, lambda g: finish(g, dpad, starts), lambda g: g, grad)
        mine = jnp.where(active, result, mine)
        grad = shifted(result, "section", -1)
        return (grad, mine)

    grad, mine = lax.fori_loop(0, sections, turn, (cotangent, mine))
    return mine[None]


def solution(mesh):
    return jax.shard_map(
        shards,
        mesh=mesh,
        in_specs=(
            P("section", "ctx", None),
            P("section", None, "ctx", None),
            P("section", "ctx", None),
            P("section", None),
            P("section", None),
            P("ctx", None),
        ),
        out_specs=P("section", "ctx", None),
        check_vma=False,
    )
```

```python
import jax
import jax.numpy as jnp
from jax import lax
from jax.experimental import pallas as pl
from jax.experimental.pallas import tpu as pltpu
from jax.sharding import PartitionSpec as P

MESH = pl.DeviceIdType.MESH
EDGE = 16
LANES = 128
TILE = 512
DEVICES = 32
GATES = {"pair": 4, "ends": 2, "inner": 5}
BEHIND = 2


def mate(c):
    return c + 1 - 2 * (c % 2)


class Spot:
    def __init__(self):
        self.level = lax.axis_index("section")
        self.me = me = lax.axis_index("ctx")
        self.z, self.q, self.p = me // 4, (me // 2) % 2, me % 2

    def ctx(self, z, q, p):
        return z * 4 + q * 2 + p


def greet(spot):
    barrier = pltpu.get_barrier_semaphore()
    index = spot.me * 2 + spot.level

    def hello(k, c):
        device = (index + k) % DEVICES
        pl.semaphore_signal(
            barrier, inc=1, device_id={"ctx": device // 2, "section": device % 2}, device_id_type=MESH
        )
        return c

    lax.fori_loop(1, DEVICES, hello, 0)
    pl.semaphore_wait(barrier, DEVICES - 1)


PAIR, SIDE, UP, DOWN = range(4)
OUTER, LAST, MIX, PLANE = range(4)


class Gather:
    def __init__(self, spot, conv, mix, conv_full, mix_full, other, send_sem, recv_sem, own_sem):
        self.spot, self.conv, self.mix, self.conv_full, self.mix_full = spot, conv, mix, conv_full, mix_full
        self.other, self.send_sem, self.recv_sem, self.own_sem = other, send_sem, recv_sem, own_sem
        self.depth, self.inner = conv.shape[2], mix.shape[1]
        self.half = conv_full.shape[1] // 3

    def taps(self, kind):
        return pl.ds(0, 2 * self.half) if kind == OUTER else pl.ds(2 * self.half, self.half)

    def full(self, kind, source):
        if kind == PLANE:
            return self.conv_full.at[pl.ds(pl.multiple_of(source * self.depth, 16), 4 * self.depth), self.taps(LAST)]
        if kind != MIX:
            rows = pl.ds(pl.multiple_of(source * self.depth, 16), self.depth)
            return self.conv_full.at[rows, self.taps(kind)]
        return self.mix_full.at[pl.ds(pl.multiple_of((source % 8) * self.inner, 16), self.inner), :]

    def leaving(self, kind, source, lane):
        z, p = source // 4, source % 2
        if kind == PLANE:
            return 41 + z + (lane == DOWN)
        if kind == LAST:
            return 38 if lane == PAIR else 39 + p
        first = 0 if kind == OUTER else 19
        if lane == PAIR:
            return first + 18
        if lane == SIDE:
            return first + 10 + 2 * z + p
        return first + 2 * (z + (lane == DOWN)) + p

    def coming(self, kind, source):
        if kind == OUTER:
            return source
        if kind == MIX:
            return 16 + source % 8
        return 24 + source % 4 if kind == LAST else 28 + source // 4

    def copy(self, kind, source, mine, lane):
        spot = self.spot
        z, q, p = spot.z, spot.q, spot.p
        device = (
            spot.ctx(z, q, 1 - p), spot.ctx(z, 1 - q, p), spot.ctx(z + 1, q, p), spot.ctx(z - 1, q, p),
        )[lane]
        here = self.full(kind, source)
        if mine and kind == MIX:
            here = self.mix.at[0]
        elif mine and lane == PAIR:
            here = self.other.at[:, self.taps(kind)]
        return pltpu.make_async_remote_copy(
            src_ref=here,
            dst_ref=self.full(kind, source),
            send_sem=self.send_sem.at[self.leaving(kind, source, lane)],
            recv_sem=self.recv_sem.at[self.coming(kind, source)],
            device_id={"ctx": device},
            device_id_type=MESH,
        )

    def send(self, kind, source, mine, lane, act):
        z = self.spot.z
        if lane == UP:
            pl.when(z < 3)(lambda: act(self.copy(kind, source, mine, lane)))
        elif lane == DOWN:
            pl.when(z > 0)(lambda: act(self.copy(kind, source, mine, lane)))
        else:
            act(self.copy(kind, source, mine, lane))

    def own(self):
        spot = self.spot
        copies = []
        for k in range(3):
            for n, p in enumerate((spot.p, 1 - spot.p)):
                cols = pl.ds(k * self.half, self.half)
                rows = pl.ds(pl.multiple_of(spot.me * self.depth, 16), self.depth)
                copies.append(
                    pltpu.make_async_copy(
                        self.conv.at[0, k, :, pl.ds(pl.multiple_of(p * self.half, 128), self.half)],
                        self.other.at[:, cols] if n else self.conv_full.at[rows, cols],
                        self.own_sem.at[k, n],
                    )
                )
        return copies

    def own_mix(self, act):
        spot = self.spot
        pl.when(spot.z // 2 == spot.p)(
            lambda: act(pltpu.make_async_copy(self.mix.at[0], self.full(MIX, spot.me), self.own_sem.at[3, 0]))
        )

    def begin_pair(self, act):
        spot = self.spot
        self.send(OUTER, spot.me, True, PAIR, act)

        @pl.when(spot.z // 2 == 1 - spot.p)
        def _():
            self.send(MIX, spot.me, True, PAIR, act)

        self.send(LAST, spot.me, True, PAIR, act)

    def begin(self, act):
        spot = self.spot
        me = spot.me
        for lane in (UP, DOWN):
            self.send(OUTER, me, True, lane, act)
        self.send(LAST, me, True, SIDE, act)

        @pl.when(spot.z // 2 == spot.p)
        def _():
            for lane in (UP, DOWN, SIDE):
                self.send(MIX, me, True, lane, act)

        self.send(OUTER, me, True, SIDE, act)

    def onward(self, kind, source, t, sign, act):
        if t == 0:
            self.send(kind, source, False, UP, act)
            self.send(kind, source, False, DOWN, act)
        else:

            @pl.when(sign < 0)
            def _():
                self.send(kind, source, False, UP, act)

            @pl.when(sign > 0)
            def _():
                self.send(kind, source, False, DOWN, act)

    def arrive(self, kind, source):
        self.copy(kind, source, False, PAIR).wait_recv()

    def each(self, t, body):
        if t == 0:
            body(0)
            return
        z = self.spot.z

        def side(b, c):
            sign = (1 - 2 * b) * (2 * (z // 2) - 1)

            @pl.when((z + sign * t >= 0) & (z + sign * t < 4))
            def _():
                body(sign)

            return c

        lax.fori_loop(0, 2, side, 0)

    def hop(self, t, sign, act, wait):
        spot = self.spot
        z, q, p = spot.z + sign * t, spot.q, spot.p
        for dp in (0, 1) if t else (1,):
            near = spot.ctx(z, q, 1 - p if dp else p)
            if wait:
                self.arrive(OUTER, near)
            self.onward(OUTER, near, t, sign, act)
            self.send(OUTER, near, False, SIDE, act)

            @pl.when(z // 2 == p)
            def _():
                if wait:
                    self.arrive(MIX, near)
                self.onward(MIX, near, t, sign, act)
                self.send(MIX, near, False, SIDE, act)

            if t == 0:
                if wait:
                    self.arrive(LAST, near)
                self.send(LAST, near, False, SIDE, act)

    def hop_last(self, t, sign, act, wait):
        spot = self.spot
        z = spot.z + sign * t
        if wait:
            self.arrive(PLANE, z * 4)
        self.onward(PLANE, z * 4, t, sign, act)

    def launch_last(self, t, act, wait):
        spot = self.spot
        for lane, ready in ((DOWN, spot.z + t == 3), (UP, spot.z == t)):

            @pl.when(ready)
            def _():
                self.send(PLANE, spot.z * 4, False, lane, act)

    def side_last(self):
        spot = self.spot
        for p in (0, 1):
            self.arrive(LAST, spot.ctx(spot.z, 1 - spot.q, p))

    def rest(self, z):
        spot = self.spot
        for p in (0, 1):
            far = spot.ctx(z, 1 - spot.q, p)
            self.arrive(OUTER, far)

            @pl.when(z // 2 == spot.p)
            def _():
                self.arrive(MIX, far)

    def sent(self):
        def act(copy):
            copy.wait_send()

        self.begin_pair(act)
        self.begin(act)
        for t in range(4):
            self.each(t, lambda sign: self.hop(t, sign, act, False))
            self.launch_last(t, act, False)
            if t:
                self.each(t, lambda sign: self.hop_last(t, sign, act, False))


class Edges:
    def __init__(self, spot, level, source, first, buffer, send_sem, recv_sem):
        self.me, self.level, self.source, self.first, self.buffer = spot.me, level, source, first, buffer
        self.send_sem, self.recv_sem = send_sem, recv_sem
        self.rows = buffer.shape[1] - 2 * EDGE
        self.same = level is spot.level
        self.section = level

    def land(self, side, slot):
        return self.buffer.at[slot, pl.ds(0 if side == 0 else EDGE + self.rows, EDGE), :]

    def sends(self, remote, local):
        for side in (0, 1):
            there = self.me < 15 if side == 0 else self.me > 0
            near = self.me + 1 if side == 0 else self.me - 1
            for slot in (0, 1):
                target = near if slot == 0 else mate(near)
                start = self.first + (self.rows - EDGE if side == 0 else 0)
                source = self.source(start)
                copy = pltpu.make_async_remote_copy(
                    src_ref=source,
                    dst_ref=self.land(side, slot),
                    send_sem=self.send_sem.at[side, slot],
                    recv_sem=self.recv_sem.at[side, slot],
                    device_id={"ctx": target, "section": self.section},
                    device_id_type=MESH,
                )
                if slot == 0 or not self.same:
                    pl.when(there)(lambda: remote(copy))
                else:
                    pl.when(there & (target != self.me))(lambda: remote(copy))
                    if local is not None:
                        pl.when(there & (target == self.me))(
                            lambda: local(
                                pltpu.make_async_copy(source, self.land(side, slot), self.recv_sem.at[side, slot])
                            )
                        )

    def start(self):
        self.sends(lambda c: c.start(), lambda c: c.start())

    def sent(self):
        self.sends(lambda c: c.wait_send(), None)

    def receive(self):
        for slot in (0, 1):
            block = self.me if slot == 0 else mate(self.me)
            for side in (0, 1):
                there = block > 0 if side == 0 else block < 15
                giver = block - 1 if side == 0 else block + 1
                land = self.land(side, slot)
                source = self.buffer.at[0, pl.ds(EDGE, EDGE), :]

                arrived = pltpu.make_async_remote_copy(
                    src_ref=source,
                    dst_ref=land,
                    send_sem=self.send_sem.at[side, slot],
                    recv_sem=self.recv_sem.at[side, slot],
                    device_id={"ctx": giver, "section": 1},
                    device_id_type=MESH,
                )
                if self.same:
                    pl.when(there & (giver != self.me))(arrived.wait_recv)
                    pl.when(there & (giver == self.me))(
                        pltpu.make_async_copy(source, land, self.recv_sem.at[side, slot]).wait
                    )
                else:
                    pl.when(there)(arrived.wait_recv)

                @pl.when(jnp.logical_not(there))
                def _():
                    land[...] = jnp.zeros(land.shape, land.dtype)


def columns(count, width, body):
    def step(n, c):
        body(pl.ds(pl.multiple_of(n * width, width), width), n)
        return c

    lax.fori_loop(0, count, step, 0)


def across(left, right):
    return lax.dot_general(left, right, (((1,), (1,)), ((), ())), preferred_element_type=jnp.float32)


def tower_kernel(
    conv_w, mix_w, inputs, scale_in, shift_in, cotangent, out,
    conv_full, mix_full, other, held, scale, shift, factor, hidden, grad, conv_sum, back, dpadded, dconv, dtotal, part_out, part_in, result,
    send_sem, recv_sem, own_sem, load_sem, hid_send, hid_recv, edge_send, edge_recv, cot_send, cot_recv, cedge_send, cedge_recv,
    grad_send, grad_recv, gedge_send, gedge_recv, part_send, part_recv, out_sem, gates,
):
    spot = Spot()
    level, me = spot.level, spot.me
    rows, wide = cotangent.shape
    half = conv_full.shape[1] // 3
    plane = wide // 4
    tall = rows + 2 * EDGE
    tiles = wide // TILE
    middle = pl.ds(EDGE, rows)
    partner = spot.ctx(spot.z, spot.q, 1 - spot.p)
    gather = Gather(spot, conv_w, mix_w, conv_full, mix_full, other, send_sem, recv_sem, own_sem)

    def start(copy):
        copy.start()

    loads = [
        pltpu.make_async_copy(inputs.at[0], held, load_sem.at[0]),
        pltpu.make_async_copy(scale_in, scale, load_sem.at[2]),
        pltpu.make_async_copy(shift_in, shift, load_sem.at[3]),
    ]
    own = gather.own()
    for copy in own + loads:
        copy.start()
    gather.own_mix(start)
    load_cot = pltpu.make_async_copy(cotangent, grad.at[0, middle, :], load_sem.at[1])
    pl.when(level == 1)(load_cot.start)
    greet(spot)
    for copy in own:
        copy.wait()

    def cot_copy():
        return pltpu.make_async_remote_copy(
            src_ref=cotangent, dst_ref=grad.at[1, middle, :], send_sem=cot_send, recv_sem=cot_recv,
            device_id={"ctx": partner}, device_id_type=MESH,
        )

    cot_edges = Edges(spot, level, lambda r: cotangent.at[pl.ds(r, EDGE), :], 0, grad, cedge_send, cedge_recv)

    ends = (spot.z == 0) | (spot.z == 3)

    @pl.when(level == 1)
    def _():
        gather.begin(start)
        gather.begin_pair(start)

    for copy in loads:
        copy.wait()

    def front(cols, _):
        gain = scale[:, cols]
        pre = held[:, cols].astype(jnp.float32) * gain + shift[:, cols]
        act, slope = gelu_parts(pre)
        hidden[0, middle, cols] = act.astype(jnp.bfloat16)
        factor[:, cols] = slope * gain

    columns(wide // LANES, LANES, front)

    def hid_copy():
        return pltpu.make_async_remote_copy(
            src_ref=hidden.at[0, middle, :], dst_ref=hidden.at[1, middle, :], send_sem=hid_send, recv_sem=hid_recv,
            device_id={"ctx": partner}, device_id_type=MESH,
        )

    edges = Edges(spot, level, lambda r: hidden.at[0, pl.ds(r, EDGE), :], EDGE, hidden, edge_send, edge_recv)

    def pair_part():
        pl.semaphore_wait(gates.at[0], 1)
        gather.begin_pair(start)
        hid_copy().start()
        edges.start()

    def rest_part():
        pl.semaphore_wait(gates.at[1], 1)
        gather.begin(start)

    @pl.when(level == 1)
    def _():
        hid_copy().start()
        edges.start()
        cot_copy().start()
        cot_edges.start()

    gather.own_mix(lambda c: c.wait())

    @pl.when((level == 0) & ends)
    def _():
        rest_part()
        pair_part()

    @pl.when((level == 0) & jnp.logical_not(ends))
    def _():
        pair_part()
        rest_part()

    def add_half(here, cols):
        off = pl.ds(pl.multiple_of(2 * here * plane, 2 * plane), 2 * plane)
        near = here is mine

        def slot(n, c):
            term = jnp.dot(hidden[n, :, off], conv_full[off, cols], preferred_element_type=jnp.float32)
            if near:
                conv_sum[n, :, cols] = term
            else:
                conv_sum[n, :, cols] += term
            return c

        lax.fori_loop(0, 2, slot, 0)

    mine = spot.z // 2

    def grad_copy(n, slot):
        cols = pl.ds(n * TILE, TILE)
        return pltpu.make_async_remote_copy(
            src_ref=result.at[:, cols],
            dst_ref=grad.at[slot, middle, cols],
            send_sem=grad_send.at[n, slot],
            recv_sem=grad_recv.at[n, slot],
            device_id={"ctx": me if slot == 0 else mate(me), "section": 0},
            device_id_type=MESH,
        )

    grad_edges = Edges(spot, 0, lambda r: result.at[pl.ds(r, EDGE), :], 0, grad, gedge_send, gedge_recv)

    def pull(n, c):
        back[n] = across(grad[n], mix_full[...])
        return c

    def open_gates(stage):
        for gate, place in ((0, "pair"), (1, "ends"), (1, "inner")):
            if stage == GATES[place]:
                who = {"pair": True, "ends": ends, "inner": jnp.logical_not(ends)}[place]

                @pl.when((level == 1) & who)
                def _():
                    pl.semaphore_signal(gates.at[gate], inc=1, device_id={"section": 0}, device_id_type=MESH)

    for t in range(4):
        gather.each(t, lambda sign: gather.hop(t, sign, start, True))
        if t == 0:
            gather.side_last()
        gather.launch_last(t, start, True)
        open_gates(t)

    for t in (1, 2):
        gather.each(t, lambda sign: gather.hop_last(t, sign, start, True))
        open_gates(3 + t)

    hid_copy().wait_recv()
    edges.receive()
    for k in range(2):
        gather.rest(2 * mine + k)
    add_half(mine, pl.ds(0, 3 * half))
    open_gates(6)
    for k in range(2):
        gather.rest(2 * (1 - mine) + k)
    add_half(1 - mine, gather.taps(OUTER))

    @pl.when(level == 1)
    def _():
        load_cot.wait()
        cot_copy().wait_recv()
        cot_edges.receive()

    @pl.when(level == 0)
    def _():
        for n in range(tiles):
            for slot in (0, 1):
                grad_copy(n, slot).wait_recv()
        grad_edges.receive()

    lax.fori_loop(0, 2, pull, 0)
    gather.each(3, lambda sign: gather.hop_last(3, sign, start, True))
    add_half(1 - mine, gather.taps(LAST))

    low, count = EDGE // 2, rows + EDGE

    def slopes(m):
        cols, c0, c1, c2 = (pl.ds(m * LANES + k * half, LANES) for k in (0, 0, 1, 2))
        for n in range(2):
            near = conv_sum[n, low - 1:low - 1 + count, c0] + conv_sum[n, low + 1:low + 1 + count, c2]
            far = conv_sum[n, low - 2:low - 2 + count, c0] + conv_sum[n, low + 2:low + 2 + count, c2]
            conv = jnp.where(level == 0, near, far) + conv_sum[n, low:low + count, c1]
            value = back[n, low:low + count, cols] * gelu_parts(conv)[1]
            dpadded[n, low:low + count, cols] = value.astype(jnp.bfloat16).astype(jnp.float32)
            there = pl.ds(n * rows, rows)
            dconv[there, c1] = dpadded[n, EDGE:EDGE + rows, cols].astype(jnp.bfloat16)
            near = dpadded[n, EDGE + 1:EDGE + 1 + rows, cols]
            far = dpadded[n, EDGE + 2:EDGE + 2 + rows, cols]
            dconv[there, c0] = jnp.where(level == 0, near, far).astype(jnp.bfloat16)
            near = dpadded[n, EDGE - 1:EDGE - 1 + rows, cols]
            far = dpadded[n, EDGE - 2:EDGE - 2 + rows, cols]
            dconv[there, c2] = jnp.where(level == 0, near, far).astype(jnp.bfloat16)

    for m in range(half // LANES):
        slopes(m)

    def part_copy(n):
        return pltpu.make_async_remote_copy(
            src_ref=part_out.at[n], dst_ref=part_in.at[n], send_sem=part_send.at[n], recv_sem=part_recv.at[n],
            device_id={"ctx": partner}, device_id_type=MESH,
        )

    def out_copy(n):
        cols = pl.ds(n * TILE, TILE)
        return pltpu.make_async_copy(result.at[:, cols], out.at[0, :, cols], out_sem.at[n])

    def settle():
        hid_copy().wait_send()
        edges.sent()
        gather.sent()

        @pl.when(level == 1)
        def _():
            cot_copy().wait_send()
            cot_edges.sent()

    for n in range(tiles + BEHIND):
        if n < tiles:
            cols = pl.ds(n * TILE, TILE)
            term = across(dconv[...], conv_full[cols, :])
            part_out[n] = term[rows:].astype(jnp.bfloat16)
            dtotal[:, cols] = term[:rows]
            part_copy(n).start()
        if n == tiles - 1:
            settle()
        m = n - BEHIND
        if m >= 0:
            cols = pl.ds(m * TILE, TILE)
            part_copy(m).wait_recv()
            dhidden = dtotal[:, cols] + part_in[m].astype(jnp.float32)
            result[:, cols] = (
                grad[0, middle, cols].astype(jnp.float32) + dhidden * factor[:, cols]
            ).astype(jnp.bfloat16)
            out_copy(m).start()

            @pl.when(level == 1)
            def _():
                grad_copy(m, 0).start()
                grad_copy(m, 1).start()

    @pl.when(level == 1)
    def _():
        grad_edges.start()
    for n in range(tiles):
        part_copy(n).wait_send()
        out_copy(n).wait()

    @pl.when(level == 1)
    def _():
        for n in range(tiles):
            for slot in (0, 1):
                grad_copy(n, slot).wait_send()
        grad_edges.sent()


def tower(layer_inputs, conv_weight, mix_weight, bn_scale, bn_shift, cotangent):
    rows, wide = cotangent.shape
    inner = conv_weight.shape[3]
    half = inner // 2
    tall = rows + 2 * EDGE
    tiles = wide // TILE
    anywhere = pl.BlockSpec(memory_space=pl.ANY)
    bf16, f32 = jnp.bfloat16, jnp.float32
    dma = pltpu.SemaphoreType.DMA
    return pl.pallas_call(
        tower_kernel,
        out_shape=jax.ShapeDtypeStruct(layer_inputs.shape, bf16),
        in_specs=[anywhere] * 6,
        out_specs=anywhere,
        scratch_shapes=[
            pltpu.VMEM((wide, 3 * half), bf16),
            pltpu.VMEM((half, wide), bf16),
            pltpu.VMEM((conv_weight.shape[2], 3 * half), bf16),
            pltpu.VMEM((rows, wide), bf16),
            pltpu.VMEM((1, wide), f32),
            pltpu.VMEM((1, wide), f32),
            pltpu.VMEM((rows, wide), f32),
            pltpu.VMEM((2, tall, wide), bf16),
            pltpu.VMEM((2, tall, wide), bf16),
            pltpu.VMEM((2, tall, 3 * half), f32),
            pltpu.VMEM((2, tall, half), f32),
            pltpu.VMEM((2, tall, half), f32),
            pltpu.VMEM((2 * rows, 3 * half), bf16),
            pltpu.VMEM((rows, wide), f32),
            pltpu.VMEM((tiles, rows, TILE), bf16),
            pltpu.VMEM((tiles, rows, TILE), bf16),
            pltpu.VMEM((rows, wide), bf16),
            dma((46,)),
            dma((32,)),
            dma((4, 2)),
            dma((4,)),
            dma,
            dma,
            dma((2, 2)),
            dma((2, 2)),
            dma,
            dma,
            dma((2, 2)),
            dma((2, 2)),
            dma((tiles, 2)),
            dma((tiles, 2)),
            dma((2, 2)),
            dma((2, 2)),
            dma((tiles,)),
            dma((tiles,)),
            dma((tiles,)),
            pltpu.SemaphoreType.REGULAR((2,)),
        ],
        compiler_params=pltpu.CompilerParams(
            collective_id=0, has_side_effects=True, vmem_limit_bytes=64 * 1024 * 1024
        ),
    )(conv_weight, mix_weight, layer_inputs, bn_scale, bn_shift, cotangent)


def extended(cells, sides, width):
    for axis, dim in sides:
        count = lax.axis_size(axis)
        ends = count - 1
        head = lax.slice_in_dim(cells, 0, width, axis=dim)
        tail = lax.slice_in_dim(cells, cells.shape[dim] - width, cells.shape[dim], axis=dim)
        cells = jnp.concatenate(
            [
                lax.ppermute(tail, axis, [(i, (i + 1) % count) for i in range(ends)]),
                cells,
                lax.ppermute(head, axis, [((i + 1) % count, i) for i in range(ends)]),
            ],
            axis=dim,
        )
    return cells


def shifted(block, axis, distance):
    devices = range(lax.axis_size(axis))
    route = [(i - distance, i) for i in devices if i - distance in devices]
    return lax.ppermute(block, axis, route)


def gelu_parts(value):
    cdf = 0.5 * (1.0 + lax.erf(value * 0.7071067811865476))
    dens = jnp.exp(-0.5 * value * value) * 0.3989422804014327
    return (value * cdf, cdf + value * dens)


def shards(layer_inputs, conv_weight, mix_weight, bn_scale, bn_shift, cotangent):
    sections = lax.axis_size("section")
    level = lax.axis_index("section")
    widest = 2 ** (sections - 1)
    if lax.axis_size("ctx") == 16 and sections == 2:
        return tower(layer_inputs, conv_weight, mix_weight, bn_scale, bn_shift, cotangent)
    conv_full = lax.all_gather(conv_weight, "ctx", axis=2, tiled=True)[0]
    mix_full = lax.all_gather(mix_weight, "ctx", axis=1, tiled=True)[0]
    rows = cotangent.shape[0]
    inner = mix_full.shape[0]
    spacing = jnp.left_shift(jnp.int32(1), level)
    pre = layer_inputs[0].astype(jnp.float32) * bn_scale[0] + bn_shift[0]
    act, slope_pre = gelu_parts(pre)
    hidden = act.astype(jnp.bfloat16)
    padded = extended(hidden, (("ctx", 0),), widest)
    conv = jnp.zeros((rows, inner), jnp.float32)
    for k in range(3):
        window = lax.dynamic_slice_in_dim(padded, widest + (k - 1) * spacing, rows, 0)
        conv = conv + jnp.dot(window, conv_full[k], preferred_element_type=jnp.float32)
    _, slope_conv = gelu_parts(conv)
    factor = slope_pre * bn_scale[0]

    def make_dconv(grad):
        back = jnp.einsum("pc,hc->ph", grad, mix_full, preferred_element_type=jnp.float32)
        return (back * slope_conv).astype(jnp.bfloat16)

    def skip_dconv(grad):
        return jnp.zeros((rows, inner), jnp.bfloat16)

    def finish(grad, dpad, starts):
        dhidden = jnp.zeros((rows, conv_full.shape[1]), jnp.float32)
        for k in range(3):
            window = lax.dynamic_slice_in_dim(dpad, starts[k], rows, 0)
            dhidden = dhidden + jnp.einsum(
                "ph,ch->pc", window, conv_full[k], preferred_element_type=jnp.float32
            )
        return (grad.astype(jnp.float32) + dhidden * factor).astype(jnp.bfloat16)

    mine = jnp.zeros_like(cotangent)

    def turn(step, carry):
        grad, mine = carry
        active = level == sections - 1 - step
        dconv = lax.cond(active, make_dconv, skip_dconv, grad)
        dpad = extended(dconv, (("ctx", 0),), widest)
        starts = [widest + (1 - k) * spacing for k in range(3)]
        result = lax.cond(active, lambda g: finish(g, dpad, starts), lambda g: g, grad)
        mine = jnp.where(active, result, mine)
        grad = shifted(result, "section", -1)
        return (grad, mine)

    grad, mine = lax.fori_loop(0, sections, turn, (cotangent, mine))
    return mine[None]


def solution(mesh):
    return jax.shard_map(
        shards,
        mesh=mesh,
        in_specs=(
            P("section", "ctx", None),
            P("section", None, "ctx", None),
            P("section", "ctx", None),
            P("section", None),
            P("section", None),
            P("ctx", None),
        ),
        out_specs=P("section", "ctx", None),
        check_vma=False,
    )
```

```python
import jax
import jax.numpy as jnp
from jax import lax
from jax.experimental import pallas as pl
from jax.experimental.pallas import tpu as pltpu
from jax.sharding import PartitionSpec as P

MESH = pl.DeviceIdType.MESH
EDGE = 16
LANES = 128
TILE = 512
DEVICES = 32
GATES = {"pair": 4, "ends": 2, "inner": 5}
BEHIND = 2


def mate(c):
    return c + 1 - 2 * (c % 2)


class Spot:
    def __init__(self):
        self.level = lax.axis_index("section")
        self.me = me = lax.axis_index("ctx")
        self.z, self.q, self.p = me // 4, (me // 2) % 2, me % 2

    def ctx(self, z, q, p):
        return z * 4 + q * 2 + p


def greet(spot):
    barrier = pltpu.get_barrier_semaphore()
    index = spot.me * 2 + spot.level

    def hello(k, c):
        device = (index + k) % DEVICES
        pl.semaphore_signal(
            barrier, inc=1, device_id={"ctx": device // 2, "section": device % 2}, device_id_type=MESH
        )
        return c

    lax.fori_loop(1, DEVICES, hello, 0)
    pl.semaphore_wait(barrier, DEVICES - 1)


PAIR, SIDE, UP, DOWN = range(4)
OUTER, LAST, MIX, PLANE = range(4)


class Gather:
    def __init__(self, spot, conv, mix, conv_full, mix_full, other, send_sem, recv_sem, own_sem):
        self.spot, self.conv, self.mix, self.conv_full, self.mix_full = spot, conv, mix, conv_full, mix_full
        self.other, self.send_sem, self.recv_sem, self.own_sem = other, send_sem, recv_sem, own_sem
        self.depth, self.inner = conv.shape[2], mix.shape[1]
        self.half = conv_full.shape[1] // 3

    def taps(self, kind):
        return pl.ds(0, 2 * self.half) if kind == OUTER else pl.ds(2 * self.half, self.half)

    def full(self, kind, source):
        if kind == PLANE:
            return self.conv_full.at[pl.ds(pl.multiple_of(source * self.depth, 16), 4 * self.depth), self.taps(LAST)]
        if kind != MIX:
            rows = pl.ds(pl.multiple_of(source * self.depth, 16), self.depth)
            return self.conv_full.at[rows, self.taps(kind)]
        return self.mix_full.at[pl.ds(pl.multiple_of((source % 8) * self.inner, 16), self.inner), :]

    def leaving(self, kind, source, lane):
        z, p = source // 4, source % 2
        if kind == PLANE:
            return 41 + z + (lane == DOWN)
        if kind == LAST:
            return 38 if lane == PAIR else 39 + p
        first = 0 if kind == OUTER else 19
        if lane == PAIR:
            return first + 18
        if lane == SIDE:
            return first + 10 + 2 * z + p
        return first + 2 * (z + (lane == DOWN)) + p

    def coming(self, kind, source):
        if kind == OUTER:
            return source
        if kind == MIX:
            return 16 + source % 8
        return 24 + source % 4 if kind == LAST else 28 + source // 4

    def copy(self, kind, source, mine, lane):
        spot = self.spot
        z, q, p = spot.z, spot.q, spot.p
        device = (
            spot.ctx(z, q, 1 - p), spot.ctx(z, 1 - q, p), spot.ctx(z + 1, q, p), spot.ctx(z - 1, q, p),
        )[lane]
        here = self.full(kind, source)
        if mine and kind == MIX:
            here = self.mix.at[0]
        elif mine and lane == PAIR:
            here = self.other.at[:, self.taps(kind)]
        return pltpu.make_async_remote_copy(
            src_ref=here,
            dst_ref=self.full(kind, source),
            send_sem=self.send_sem.at[self.leaving(kind, source, lane)],
            recv_sem=self.recv_sem.at[self.coming(kind, source)],
            device_id={"ctx": device},
            device_id_type=MESH,
        )

    def send(self, kind, source, mine, lane, act):
        z = self.spot.z
        if lane == UP:
            pl.when(z < 3)(lambda: act(self.copy(kind, source, mine, lane)))
        elif lane == DOWN:
            pl.when(z > 0)(lambda: act(self.copy(kind, source, mine, lane)))
        else:
            act(self.copy(kind, source, mine, lane))

    def own(self):
        spot = self.spot
        copies = []
        for k in range(3):
            for n, p in enumerate((spot.p, 1 - spot.p)):
                cols = pl.ds(k * self.half, self.half)
                rows = pl.ds(pl.multiple_of(spot.me * self.depth, 16), self.depth)
                copies.append(
                    pltpu.make_async_copy(
                        self.conv.at[0, k, :, pl.ds(pl.multiple_of(p * self.half, 128), self.half)],
                        self.other.at[:, cols] if n else self.conv_full.at[rows, cols],
                        self.own_sem.at[k, n],
                    )
                )
        return copies

    def own_mix(self, act):
        spot = self.spot
        pl.when(spot.z // 2 == spot.p)(
            lambda: act(pltpu.make_async_copy(self.mix.at[0], self.full(MIX, spot.me), self.own_sem.at[3, 0]))
        )

    def begin_pair(self, act):
        spot = self.spot
        self.send(OUTER, spot.me, True, PAIR, act)

        @pl.when(spot.z // 2 == 1 - spot.p)
        def _():
            self.send(MIX, spot.me, True, PAIR, act)

        self.send(LAST, spot.me, True, PAIR, act)

    def begin(self, act):
        spot = self.spot
        me = spot.me
        for lane in (UP, DOWN):
            self.send(OUTER, me, True, lane, act)
        self.send(LAST, me, True, SIDE, act)

        @pl.when(spot.z // 2 == spot.p)
        def _():
            for lane in (UP, DOWN, SIDE):
                self.send(MIX, me, True, lane, act)

        self.send(OUTER, me, True, SIDE, act)

    def onward(self, kind, source, t, sign, act):
        if t == 0:
            self.send(kind, source, False, UP, act)
            self.send(kind, source, False, DOWN, act)
        else:

            @pl.when(sign < 0)
            def _():
                self.send(kind, source, False, UP, act)

            @pl.when(sign > 0)
            def _():
                self.send(kind, source, False, DOWN, act)

    def arrive(self, kind, source):
        self.copy(kind, source, False, PAIR).wait_recv()

    def each(self, t, body):
        if t == 0:
            body(0)
            return
        z = self.spot.z

        def side(b, c):
            sign = (1 - 2 * b) * (2 * (z // 2) - 1)

            @pl.when((z + sign * t >= 0) & (z + sign * t < 4))
            def _():
                body(sign)

            return c

        lax.fori_loop(0, 2, side, 0)

    def hop(self, t, sign, act, wait):
        spot = self.spot
        z, q, p = spot.z + sign * t, spot.q, spot.p
        for dp in (0, 1) if t else (1,):
            near = spot.ctx(z, q, 1 - p if dp else p)
            if wait:
                self.arrive(OUTER, near)
            self.onward(OUTER, near, t, sign, act)
            self.send(OUTER, near, False, SIDE, act)

            @pl.when(z // 2 == p)
            def _():
                if wait:
                    self.arrive(MIX, near)
                self.onward(MIX, near, t, sign, act)
                self.send(MIX, near, False, SIDE, act)

            if t == 0:
                if wait:
                    self.arrive(LAST, near)
                self.send(LAST, near, False, SIDE, act)

    def hop_last(self, t, sign, act, wait):
        spot = self.spot
        z = spot.z + sign * t
        if wait:
            self.arrive(PLANE, z * 4)
        self.onward(PLANE, z * 4, t, sign, act)

    def launch_last(self, t, act, wait):
        spot = self.spot
        for lane, ready in ((DOWN, ((spot.z == 3) & (t == 0)) | ((spot.z < 3) & (t == 1))), (UP, ((spot.z == 0) & (t == 0)) | ((spot.z > 0) & (t == 1)))):

            @pl.when(ready)
            def _():
                self.send(PLANE, spot.z * 4, False, lane, act)

    def side_last(self):
        spot = self.spot
        for p in (0, 1):
            self.arrive(LAST, spot.ctx(spot.z, 1 - spot.q, p))

    def rest(self, z):
        spot = self.spot
        for p in (0, 1):
            far = spot.ctx(z, 1 - spot.q, p)
            self.arrive(OUTER, far)

            @pl.when(z // 2 == spot.p)
            def _():
                self.arrive(MIX, far)

    def sent(self):
        def act(copy):
            copy.wait_send()

        self.begin_pair(act)
        self.begin(act)
        for t in range(4):
            self.each(t, lambda sign: self.hop(t, sign, act, False))
            self.launch_last(t, act, False)
            if t:
                self.each(t, lambda sign: self.hop_last(t, sign, act, False))


class Edges:
    def __init__(self, spot, level, source, first, buffer, send_sem, recv_sem):
        self.me, self.level, self.source, self.first, self.buffer = spot.me, level, source, first, buffer
        self.send_sem, self.recv_sem = send_sem, recv_sem
        self.rows = buffer.shape[1] - 2 * EDGE
        self.same = level is spot.level
        self.section = level

    def land(self, side, slot):
        return self.buffer.at[slot, pl.ds(0 if side == 0 else EDGE + self.rows, EDGE), :]

    def sends(self, remote, local):
        for side in (0, 1):
            there = self.me < 15 if side == 0 else self.me > 0
            near = self.me + 1 if side == 0 else self.me - 1
            for slot in (0, 1):
                target = near if slot == 0 else mate(near)
                start = self.first + (self.rows - EDGE if side == 0 else 0)
                source = self.source(start)
                copy = pltpu.make_async_remote_copy(
                    src_ref=source,
                    dst_ref=self.land(side, slot),
                    send_sem=self.send_sem.at[side, slot],
                    recv_sem=self.recv_sem.at[side, slot],
                    device_id={"ctx": target, "section": self.section},
                    device_id_type=MESH,
                )
                if slot == 0 or not self.same:
                    pl.when(there)(lambda: remote(copy))
                else:
                    pl.when(there & (target != self.me))(lambda: remote(copy))
                    if local is not None:
                        pl.when(there & (target == self.me))(
                            lambda: local(
                                pltpu.make_async_copy(source, self.land(side, slot), self.recv_sem.at[side, slot])
                            )
                        )

    def start(self):
        self.sends(lambda c: c.start(), lambda c: c.start())

    def sent(self):
        self.sends(lambda c: c.wait_send(), None)

    def receive(self):
        for slot in (0, 1):
            block = self.me if slot == 0 else mate(self.me)
            for side in (0, 1):
                there = block > 0 if side == 0 else block < 15
                giver = block - 1 if side == 0 else block + 1
                land = self.land(side, slot)
                source = self.buffer.at[0, pl.ds(EDGE, EDGE), :]

                arrived = pltpu.make_async_remote_copy(
                    src_ref=source,
                    dst_ref=land,
                    send_sem=self.send_sem.at[side, slot],
                    recv_sem=self.recv_sem.at[side, slot],
                    device_id={"ctx": giver, "section": 1},
                    device_id_type=MESH,
                )
                if self.same:
                    pl.when(there & (giver != self.me))(arrived.wait_recv)
                    pl.when(there & (giver == self.me))(
                        pltpu.make_async_copy(source, land, self.recv_sem.at[side, slot]).wait
                    )
                else:
                    pl.when(there)(arrived.wait_recv)

                @pl.when(jnp.logical_not(there))
                def _():
                    land[...] = jnp.zeros(land.shape, land.dtype)


def columns(count, width, body):
    def step(n, c):
        body(pl.ds(pl.multiple_of(n * width, width), width), n)
        return c

    lax.fori_loop(0, count, step, 0)


def across(left, right):
    return lax.dot_general(left, right, (((1,), (1,)), ((), ())), preferred_element_type=jnp.float32)


def tower_kernel(
    conv_w, mix_w, inputs, scale_in, shift_in, cotangent, out,
    conv_full, mix_full, other, held, scale, shift, factor, hidden, grad, conv_sum, back, dpadded, dconv, dtotal, part_out, part_in, result,
    send_sem, recv_sem, own_sem, load_sem, hid_send, hid_recv, edge_send, edge_recv, cot_send, cot_recv, cedge_send, cedge_recv,
    grad_send, grad_recv, gedge_send, gedge_recv, part_send, part_recv, out_sem, gates,
):
    spot = Spot()
    level, me = spot.level, spot.me
    rows, wide = cotangent.shape
    half = conv_full.shape[1] // 3
    plane = wide // 4
    tall = rows + 2 * EDGE
    tiles = wide // TILE
    middle = pl.ds(EDGE, rows)
    partner = spot.ctx(spot.z, spot.q, 1 - spot.p)
    gather = Gather(spot, conv_w, mix_w, conv_full, mix_full, other, send_sem, recv_sem, own_sem)

    def start(copy):
        copy.start()

    loads = [
        pltpu.make_async_copy(inputs.at[0], held, load_sem.at[0]),
        pltpu.make_async_copy(scale_in, scale, load_sem.at[2]),
        pltpu.make_async_copy(shift_in, shift, load_sem.at[3]),
    ]
    own = gather.own()
    for copy in own + loads:
        copy.start()
    gather.own_mix(start)
    load_cot = pltpu.make_async_copy(cotangent, grad.at[0, middle, :], load_sem.at[1])
    pl.when(level == 1)(load_cot.start)
    greet(spot)
    for copy in own:
        copy.wait()

    def cot_copy():
        return pltpu.make_async_remote_copy(
            src_ref=cotangent, dst_ref=grad.at[1, middle, :], send_sem=cot_send, recv_sem=cot_recv,
            device_id={"ctx": partner}, device_id_type=MESH,
        )

    cot_edges = Edges(spot, level, lambda r: cotangent.at[pl.ds(r, EDGE), :], 0, grad, cedge_send, cedge_recv)

    ends = (spot.z == 0) | (spot.z == 3)

    @pl.when(level == 1)
    def _():
        gather.begin(start)
        gather.begin_pair(start)

    for copy in loads:
        copy.wait()

    def front(cols, _):
        gain = scale[:, cols]
        pre = held[:, cols].astype(jnp.float32) * gain + shift[:, cols]
        act, slope = gelu_parts(pre)
        hidden[0, middle, cols] = act.astype(jnp.bfloat16)
        factor[:, cols] = slope * gain

    columns(wide // LANES, LANES, front)

    def hid_copy():
        return pltpu.make_async_remote_copy(
            src_ref=hidden.at[0, middle, :], dst_ref=hidden.at[1, middle, :], send_sem=hid_send, recv_sem=hid_recv,
            device_id={"ctx": partner}, device_id_type=MESH,
        )

    edges = Edges(spot, level, lambda r: hidden.at[0, pl.ds(r, EDGE), :], EDGE, hidden, edge_send, edge_recv)

    def pair_part():
        pl.semaphore_wait(gates.at[0], 1)
        gather.begin_pair(start)
        hid_copy().start()
        edges.start()

    def rest_part():
        pl.semaphore_wait(gates.at[1], 1)
        gather.begin(start)

    @pl.when(level == 1)
    def _():
        hid_copy().start()
        edges.start()
        cot_copy().start()
        cot_edges.start()

    gather.own_mix(lambda c: c.wait())

    @pl.when((level == 0) & ends)
    def _():
        rest_part()
        pair_part()

    @pl.when((level == 0) & jnp.logical_not(ends))
    def _():
        pair_part()
        rest_part()

    def add_half(here, cols):
        off = pl.ds(pl.multiple_of(2 * here * plane, 2 * plane), 2 * plane)
        near = here is mine

        def slot(n, c):
            term = jnp.dot(hidden[n, :, off], conv_full[off, cols], preferred_element_type=jnp.float32)
            if near:
                conv_sum[n, :, cols] = term
            else:
                conv_sum[n, :, cols] += term
            return c

        lax.fori_loop(0, 2, slot, 0)

    mine = spot.z // 2

    def grad_copy(n, slot):
        cols = pl.ds(n * TILE, TILE)
        return pltpu.make_async_remote_copy(
            src_ref=result.at[:, cols],
            dst_ref=grad.at[slot, middle, cols],
            send_sem=grad_send.at[n, slot],
            recv_sem=grad_recv.at[n, slot],
            device_id={"ctx": me if slot == 0 else mate(me), "section": 0},
            device_id_type=MESH,
        )

    grad_edges = Edges(spot, 0, lambda r: result.at[pl.ds(r, EDGE), :], 0, grad, gedge_send, gedge_recv)

    def pull(n, c):
        back[n] = across(grad[n], mix_full[...])
        return c

    def open_gates(stage):
        for gate, place in ((0, "pair"), (1, "ends"), (1, "inner")):
            if stage == GATES[place]:
                who = {"pair": True, "ends": ends, "inner": jnp.logical_not(ends)}[place]

                @pl.when((level == 1) & who)
                def _():
                    pl.semaphore_signal(gates.at[gate], inc=1, device_id={"section": 0}, device_id_type=MESH)

    for t in range(4):
        gather.each(t, lambda sign: gather.hop(t, sign, start, True))
        if t == 0:
            gather.side_last()
        gather.launch_last(t, start, True)
        open_gates(t)

    for t in (1, 2):
        gather.each(t, lambda sign: gather.hop_last(t, sign, start, True))
        open_gates(3 + t)

    hid_copy().wait_recv()
    edges.receive()
    for k in range(2):
        gather.rest(2 * mine + k)
    add_half(mine, pl.ds(0, 3 * half))
    open_gates(6)
    for k in range(2):
        gather.rest(2 * (1 - mine) + k)
    add_half(1 - mine, gather.taps(OUTER))

    @pl.when(level == 1)
    def _():
        load_cot.wait()
        cot_copy().wait_recv()
        cot_edges.receive()

    @pl.when(level == 0)
    def _():
        for n in range(tiles):
            for slot in (0, 1):
                grad_copy(n, slot).wait_recv()
        grad_edges.receive()

    lax.fori_loop(0, 2, pull, 0)
    gather.each(3, lambda sign: gather.hop_last(3, sign, start, True))
    add_half(1 - mine, gather.taps(LAST))

    low, count = EDGE // 2, rows + EDGE

    def slopes(m):
        cols, c0, c1, c2 = (pl.ds(m * LANES + k * half, LANES) for k in (0, 0, 1, 2))
        for n in range(2):
            near = conv_sum[n, low - 1:low - 1 + count, c0] + conv_sum[n, low + 1:low + 1 + count, c2]
            far = conv_sum[n, low - 2:low - 2 + count, c0] + conv_sum[n, low + 2:low + 2 + count, c2]
            conv = jnp.where(level == 0, near, far) + conv_sum[n, low:low + count, c1]
            value = back[n, low:low + count, cols] * gelu_parts(conv)[1]
            dpadded[n, low:low + count, cols] = value.astype(jnp.bfloat16).astype(jnp.float32)
            there = pl.ds(n * rows, rows)
            dconv[there, c1] = dpadded[n, EDGE:EDGE + rows, cols].astype(jnp.bfloat16)
            near = dpadded[n, EDGE + 1:EDGE + 1 + rows, cols]
            far = dpadded[n, EDGE + 2:EDGE + 2 + rows, cols]
            dconv[there, c0] = jnp.where(level == 0, near, far).astype(jnp.bfloat16)
            near = dpadded[n, EDGE - 1:EDGE - 1 + rows, cols]
            far = dpadded[n, EDGE - 2:EDGE - 2 + rows, cols]
            dconv[there, c2] = jnp.where(level == 0, near, far).astype(jnp.bfloat16)

    for m in range(half // LANES):
        slopes(m)

    def part_copy(n):
        return pltpu.make_async_remote_copy(
            src_ref=part_out.at[n], dst_ref=part_in.at[n], send_sem=part_send.at[n], recv_sem=part_recv.at[n],
            device_id={"ctx": partner}, device_id_type=MESH,
        )

    def out_copy(n):
        cols = pl.ds(n * TILE, TILE)
        return pltpu.make_async_copy(result.at[:, cols], out.at[0, :, cols], out_sem.at[n])

    def settle():
        hid_copy().wait_send()
        edges.sent()
        gather.sent()

        @pl.when(level == 1)
        def _():
            cot_copy().wait_send()
            cot_edges.sent()

    for n in range(tiles + BEHIND):
        if n < tiles:
            cols = pl.ds(n * TILE, TILE)
            term = across(dconv[...], conv_full[cols, :])
            part_out[n] = term[rows:].astype(jnp.bfloat16)
            dtotal[:, cols] = term[:rows]
            part_copy(n).start()
        if n == tiles - 1:
            settle()
        m = n - BEHIND
        if m >= 0:
            cols = pl.ds(m * TILE, TILE)
            part_copy(m).wait_recv()
            dhidden = dtotal[:, cols] + part_in[m].astype(jnp.float32)
            result[:, cols] = (
                grad[0, middle, cols].astype(jnp.float32) + dhidden * factor[:, cols]
            ).astype(jnp.bfloat16)
            out_copy(m).start()

            @pl.when(level == 1)
            def _():
                grad_copy(m, 0).start()
                grad_copy(m, 1).start()

    @pl.when(level == 1)
    def _():
        grad_edges.start()
    for n in range(tiles):
        part_copy(n).wait_send()
        out_copy(n).wait()

    @pl.when(level == 1)
    def _():
        for n in range(tiles):
            for slot in (0, 1):
                grad_copy(n, slot).wait_send()
        grad_edges.sent()


def tower(layer_inputs, conv_weight, mix_weight, bn_scale, bn_shift, cotangent):
    rows, wide = cotangent.shape
    inner = conv_weight.shape[3]
    half = inner // 2
    tall = rows + 2 * EDGE
    tiles = wide // TILE
    anywhere = pl.BlockSpec(memory_space=pl.ANY)
    bf16, f32 = jnp.bfloat16, jnp.float32
    dma = pltpu.SemaphoreType.DMA
    return pl.pallas_call(
        tower_kernel,
        out_shape=jax.ShapeDtypeStruct(layer_inputs.shape, bf16),
        in_specs=[anywhere] * 6,
        out_specs=anywhere,
        scratch_shapes=[
            pltpu.VMEM((wide, 3 * half), bf16),
            pltpu.VMEM((half, wide), bf16),
            pltpu.VMEM((conv_weight.shape[2], 3 * half), bf16),
            pltpu.VMEM((rows, wide), bf16),
            pltpu.VMEM((1, wide), f32),
            pltpu.VMEM((1, wide), f32),
            pltpu.VMEM((rows, wide), f32),
            pltpu.VMEM((2, tall, wide), bf16),
            pltpu.VMEM((2, tall, wide), bf16),
            pltpu.VMEM((2, tall, 3 * half), f32),
            pltpu.VMEM((2, tall, half), f32),
            pltpu.VMEM((2, tall, half), f32),
            pltpu.VMEM((2 * rows, 3 * half), bf16),
            pltpu.VMEM((rows, wide), f32),
            pltpu.VMEM((tiles, rows, TILE), bf16),
            pltpu.VMEM((tiles, rows, TILE), bf16),
            pltpu.VMEM((rows, wide), bf16),
            dma((46,)),
            dma((32,)),
            dma((4, 2)),
            dma((4,)),
            dma,
            dma,
            dma((2, 2)),
            dma((2, 2)),
            dma,
            dma,
            dma((2, 2)),
            dma((2, 2)),
            dma((tiles, 2)),
            dma((tiles, 2)),
            dma((2, 2)),
            dma((2, 2)),
            dma((tiles,)),
            dma((tiles,)),
            dma((tiles,)),
            pltpu.SemaphoreType.REGULAR((2,)),
        ],
        compiler_params=pltpu.CompilerParams(
            collective_id=0, has_side_effects=True, vmem_limit_bytes=64 * 1024 * 1024
        ),
    )(conv_weight, mix_weight, layer_inputs, bn_scale, bn_shift, cotangent)


def extended(cells, sides, width):
    for axis, dim in sides:
        count = lax.axis_size(axis)
        ends = count - 1
        head = lax.slice_in_dim(cells, 0, width, axis=dim)
        tail = lax.slice_in_dim(cells, cells.shape[dim] - width, cells.shape[dim], axis=dim)
        cells = jnp.concatenate(
            [
                lax.ppermute(tail, axis, [(i, (i + 1) % count) for i in range(ends)]),
                cells,
                lax.ppermute(head, axis, [((i + 1) % count, i) for i in range(ends)]),
            ],
            axis=dim,
        )
    return cells


def shifted(block, axis, distance):
    devices = range(lax.axis_size(axis))
    route = [(i - distance, i) for i in devices if i - distance in devices]
    return lax.ppermute(block, axis, route)


def gelu_parts(value):
    cdf = 0.5 * (1.0 + lax.erf(value * 0.7071067811865476))
    dens = jnp.exp(-0.5 * value * value) * 0.3989422804014327
    return (value * cdf, cdf + value * dens)


def shards(layer_inputs, conv_weight, mix_weight, bn_scale, bn_shift, cotangent):
    sections = lax.axis_size("section")
    level = lax.axis_index("section")
    widest = 2 ** (sections - 1)
    if lax.axis_size("ctx") == 16 and sections == 2:
        return tower(layer_inputs, conv_weight, mix_weight, bn_scale, bn_shift, cotangent)
    conv_full = lax.all_gather(conv_weight, "ctx", axis=2, tiled=True)[0]
    mix_full = lax.all_gather(mix_weight, "ctx", axis=1, tiled=True)[0]
    rows = cotangent.shape[0]
    inner = mix_full.shape[0]
    spacing = jnp.left_shift(jnp.int32(1), level)
    pre = layer_inputs[0].astype(jnp.float32) * bn_scale[0] + bn_shift[0]
    act, slope_pre = gelu_parts(pre)
    hidden = act.astype(jnp.bfloat16)
    padded = extended(hidden, (("ctx", 0),), widest)
    conv = jnp.zeros((rows, inner), jnp.float32)
    for k in range(3):
        window = lax.dynamic_slice_in_dim(padded, widest + (k - 1) * spacing, rows, 0)
        conv = conv + jnp.dot(window, conv_full[k], preferred_element_type=jnp.float32)
    _, slope_conv = gelu_parts(conv)
    factor = slope_pre * bn_scale[0]

    def make_dconv(grad):
        back = jnp.einsum("pc,hc->ph", grad, mix_full, preferred_element_type=jnp.float32)
        return (back * slope_conv).astype(jnp.bfloat16)

    def skip_dconv(grad):
        return jnp.zeros((rows, inner), jnp.bfloat16)

    def finish(grad, dpad, starts):
        dhidden = jnp.zeros((rows, conv_full.shape[1]), jnp.float32)
        for k in range(3):
            window = lax.dynamic_slice_in_dim(dpad, starts[k], rows, 0)
            dhidden = dhidden + jnp.einsum(
                "ph,ch->pc", window, conv_full[k], preferred_element_type=jnp.float32
            )
        return (grad.astype(jnp.float32) + dhidden * factor).astype(jnp.bfloat16)

    mine = jnp.zeros_like(cotangent)

    def turn(step, carry):
        grad, mine = carry
        active = level == sections - 1 - step
        dconv = lax.cond(active, make_dconv, skip_dconv, grad)
        dpad = extended(dconv, (("ctx", 0),), widest)
        starts = [widest + (1 - k) * spacing for k in range(3)]
        result = lax.cond(active, lambda g: finish(g, dpad, starts), lambda g: g, grad)
        mine = jnp.where(active, result, mine)
        grad = shifted(result, "section", -1)
        return (grad, mine)

    grad, mine = lax.fori_loop(0, sections, turn, (cotangent, mine))
    return mine[None]


def solution(mesh):
    return jax.shard_map(
        shards,
        mesh=mesh,
        in_specs=(
            P("section", "ctx", None),
            P("section", None, "ctx", None),
            P("section", "ctx", None),
            P("section", None),
            P("section", None),
            P("ctx", None),
        ),
        out_specs=P("section", "ctx", None),
        check_vma=False,
    )
```
